32 devices in a mesh: groups: 2 (over x), frame: 16 (over z, y, core).
Axes of the slice: x: 2, y: 2, z: 4, core: 2. Of those that a mesh axis runs over, the one named last changes fastest.
Arguments:
- video_qkv: bfloat16 [3, 32, 128, 1536], P(None, ('groups', 'frame')), parts along dimension 1, may hold values from -8 to 8
- text_qkv: bfloat16 [3, 512, 1536], P(None, ('groups', 'frame')), parts along dimension 1, may hold values from -8 to 8
- head_kind: int32 [24], P('groups'), parts along dimension 0, may hold values from 0 to 1, as said below
- text_len: int32 [2], P('groups'), parts along dimension 0, may hold values from 64 to 256
Outputs:
- video_out: bfloat16 [32, 128, 1536], P(('groups', 'frame')), parts along dimension 0
- text_out: bfloat16 [512, 1536], P(('groups', 'frame')), parts along dimension 0
The draws below stay inside these ranges and needn't reach their ends.
There are 2 independent parts, one for each index of `groups`. The reference program is written for one: setup_inputs(seed, part) draws one part's arguments, and reference() takes and returns one part's arrays. A program takes and returns all parts, laid end to end along the dimension named above; each array names one. Nothing has to cross between parts.
Inputs may be any that keep to these rules, and one draw needn't show every extreme that they name: `head_kind`: exactly 6 of the 12 entries are 1.
All inputs are finite; a program needn't handle non-finite values.
Results may differ from the reference program's by a relative error of at most 0.009.
Values may be sent and summed in bfloat16 or wider, within the bound.
A program may use at most 448 MiB of HBM per device.

```python
import jax
import jax.numpy as jnp
from jax import lax

H = 12
HD = 128
TXT = 256
P_SIZE = 128
FRAMES = 16
HT = 6


def rough_values(key, full_shape):
    base_key = jax.random.fold_in(key, 11)
    drawn = jnp.clip(jax.random.normal(base_key, full_shape, jnp.float32), -6.0, 6.0)
    return drawn


def draw_video_qkv(key, part):
    full_shape = (3, FRAMES, P_SIZE, H * HD)
    drawn = rough_values(jax.random.fold_in(key, 21), full_shape)
    return drawn.astype(jnp.bfloat16)


def draw_text_qkv(key, part):
    full_shape = (3, TXT, H * HD)
    drawn = rough_values(jax.random.fold_in(key, 31), full_shape)
    return drawn.astype(jnp.bfloat16)


def draw_head_kind(key, part):
    shuffled = jax.random.permutation(jax.random.fold_in(key, 3), H)
    return (shuffled < HT).astype(jnp.int32)


def setup_inputs(seed: int = 0, part: int = 0) -> dict:
    key_of = jax.random.split(jax.random.key(seed), 5)
    part_splits = jax.random.split(jax.random.fold_in(key_of[4], part), 5)
    video_qkv = draw_video_qkv(jax.random.fold_in(jax.random.fold_in(key_of[4], part), 71), part)
    text_qkv = draw_text_qkv(jax.random.fold_in(jax.random.fold_in(key_of[4], part), 71), part)
    head_kind = draw_head_kind(jax.random.fold_in(jax.random.fold_in(key_of[4], part), 71), part)
    text_len = jax.random.randint(part_splits[3], (1,), TXT // 4, TXT + 1).astype(jnp.int32)
    return {"video_qkv": video_qkv, "text_qkv": text_qkv, "head_kind": head_kind, "text_len": text_len}


masked_score = -1e30


def reference(video_qkv, text_qkv, head_kind, text_len):
    video = video_qkv.reshape(3, FRAMES, P_SIZE, H, HD)
    texts = text_qkv.reshape(3, TXT, H, HD)
    score_scale = HD ** -0.5
    text_valid = jnp.arange(TXT) < text_len[0]
    spatial_heads = jnp.nonzero(head_kind == 0, size=H - HT)[0].astype(jnp.int32)
    temporal_heads = jnp.nonzero(head_kind == 1, size=HT)[0].astype(jnp.int32)
    video_spatial = jnp.take(video, spatial_heads, axis=3)
    text_spatial = jnp.take(texts, spatial_heads, axis=2)
    text_keys_sp = text_spatial[1].astype(jnp.float32)
    text_values_sp = text_spatial[2].astype(jnp.float32)

    def spatial_frame(frame_block):
        queries = frame_block[0].astype(jnp.float32)
        own_scores = jnp.einsum("phd,khd->hpk", queries, frame_block[1].astype(jnp.float32)) * score_scale
        text_scores = jnp.einsum("phd,khd->hpk", queries, text_keys_sp) * score_scale
        text_scores = jnp.where(text_valid, text_scores, masked_score)
        row_max = jnp.maximum(own_scores.max(-1), text_scores.max(-1))[..., None]
        own_exp = jnp.exp(own_scores - row_max)
        text_exp = jnp.exp(text_scores - row_max)
        totals = own_exp.sum(-1) + text_exp.sum(-1)
        own_weight = lax.optimization_barrier(own_exp.astype(jnp.bfloat16)).astype(jnp.float32)
        text_weight = lax.optimization_barrier(text_exp.astype(jnp.bfloat16)).astype(jnp.float32)
        summed = jnp.einsum("hpk,khd->phd", own_weight, frame_block[2].astype(jnp.float32))
        summed = summed + jnp.einsum("hpk,khd->phd", text_weight, text_values_sp)
        return summed / totals.T[..., None]

    spatial_out = lax.map(spatial_frame, jnp.moveaxis(video_spatial, 1, 0))
    video_temporal = jnp.moveaxis(jnp.take(video, temporal_heads, axis=3), 3, 0)

    def temporal_head(head_block):
        queries = head_block[0].astype(jnp.float32)
        scores = jnp.einsum("fpd,gpd->pfg", queries, head_block[1].astype(jnp.float32)) * score_scale
        row_max = scores.max(-1, keepdims=True)
        exps = jnp.exp(scores - row_max)
        totals = exps.sum(-1)
        weight = lax.optimization_barrier(exps.astype(jnp.bfloat16)).astype(jnp.float32)
        summed = jnp.einsum("pfg,gpd->fpd", weight, head_block[2].astype(jnp.float32))
        return summed / totals.T[..., None]

    temporal_out = jnp.moveaxis(lax.map(temporal_head, video_temporal), 0, 2)
    joined = jnp.concatenate([spatial_out, temporal_out], axis=2)
    order = jnp.concatenate([spatial_heads, temporal_heads]).astype(jnp.int32)
    inverse = jnp.argsort(order).astype(jnp.int32)
    video_out = jnp.take(joined, inverse, axis=2).astype(jnp.bfloat16).reshape(FRAMES, P_SIZE, H * HD)

    flat_keys = video[1].reshape(FRAMES * P_SIZE, H, HD)
    flat_values = video[2].reshape(FRAMES * P_SIZE, H, HD)

    def text_head(head_index):
        queries = texts[0][:, head_index]
        text_scores = jnp.dot(queries, texts[1][:, head_index].T, preferred_element_type=jnp.float32) * score_scale
        text_scores = jnp.where(text_valid, text_scores, masked_score)
        video_scores = jnp.dot(queries, flat_keys[:, head_index].T, preferred_element_type=jnp.float32) * score_scale
        row_max = jnp.maximum(text_scores.max(-1), video_scores.max(-1))[:, None]
        text_exp = jnp.exp(text_scores - row_max)
        video_exp = jnp.exp(video_scores - row_max)
        totals = text_exp.sum(-1) + video_exp.sum(-1)
        summed = jnp.dot(text_exp.astype(jnp.bfloat16), texts[2][:, head_index], preferred_element_type=jnp.float32)
        summed = summed + jnp.dot(video_exp.astype(jnp.bfloat16), flat_values[:, head_index], preferred_element_type=jnp.float32)
        return summed / totals[:, None]

    text_all = lax.map(text_head, jnp.arange(H, dtype=jnp.int32))
    text_out = jnp.moveaxis(text_all, 0, 1).astype(jnp.bfloat16).reshape(TXT, H * HD)
    return video_out, text_out
```

```python
import functools

import jax
import jax.numpy as jnp
from jax import lax
from jax.experimental import pallas as pl
from jax.experimental.pallas import tpu as pltpu
from jax.sharding import PartitionSpec as P

masked_score = -1e30


def plain_body(video_qkv, text_qkv, head_kind, text_len):
    head_count = head_kind.shape[0]
    head_width = video_qkv.shape[-1]
    head_dim = head_width // head_count
    positions = video_qkv.shape[2]
    shard_text = text_qkv.shape[1]
    score_scale = head_dim ** (-0.5)
    device_rank = lax.axis_index("frame")
    local_video = video_qkv.reshape(3, 1, positions, head_count, head_dim)
    gathered = lax.all_gather(text_qkv, "frame", axis=1, tiled=True)
    text_total = gathered.shape[1]
    all_text = gathered.reshape(3, text_total, head_count, head_dim)
    text_valid = jnp.arange(text_total) < text_len[0]
    spatial_heads = jnp.nonzero(head_kind == 0, size=head_count - head_count // 2)[0].astype(
        jnp.int32
    )
    temporal_heads = jnp.nonzero(head_kind == 1, size=head_count // 2)[0].astype(jnp.int32)
    own_frame = jnp.take(local_video[:, 0], spatial_heads, axis=2)
    text_spatial = jnp.take(all_text[1:], spatial_heads, axis=2)
    joint_keys = jnp.concatenate([own_frame[1], text_spatial[0]], axis=0)
    joint_values = jnp.concatenate([own_frame[2], text_spatial[1]], axis=0)
    joint_valid = jnp.concatenate([jnp.ones((positions,), bool), text_valid])
    spatial_scores = (
        jnp.einsum("phd,khd->hpk", own_frame[0], joint_keys, preferred_element_type=jnp.float32)
        * score_scale
    )
    spatial_scores = jnp.where(joint_valid, spatial_scores, masked_score)
    row_max = spatial_scores.max(-1, keepdims=True)
    spatial_exp = jnp.exp(spatial_scores - row_max)
    totals = spatial_exp.sum(-1)
    summed = jnp.einsum(
        "hpk,khd->phd",
        spatial_exp.astype(jnp.bfloat16),
        joint_values,
        preferred_element_type=jnp.float32,
    )
    spatial_result = (summed / totals.T[..., None]).astype(jnp.bfloat16)
    selected = jnp.take(local_video, temporal_heads, axis=3)
    block = lax.all_to_all(selected, "frame", split_axis=2, concat_axis=1, tiled=True)
    scores = (
        jnp.einsum("fphd,gphd->phfg", block[0], block[1], preferred_element_type=jnp.float32)
        * score_scale
    )
    block_max = scores.max(-1, keepdims=True)
    exps = jnp.exp(scores - block_max)
    block_totals = exps.sum(-1)
    block_sum = jnp.einsum(
        "phfg,gphd->fphd", exps.astype(jnp.bfloat16), block[2], preferred_element_type=jnp.float32
    )
    result = (block_sum / jnp.transpose(block_totals, (2, 0, 1))[..., None]).astype(jnp.bfloat16)
    temporal_result = lax.all_to_all(result, "frame", split_axis=0, concat_axis=1, tiled=True)[0]
    joined = jnp.concatenate([spatial_result, temporal_result], axis=1)
    order = jnp.concatenate([spatial_heads, temporal_heads])
    inverse = jnp.argsort(order)
    video_out = jnp.take(joined, inverse, axis=1).reshape(1, positions, head_width)
    text_queries = all_text[0]
    own_text = text_qkv.reshape(3, shard_text, head_count, head_dim)
    own_valid = device_rank * shard_text + jnp.arange(shard_text) < text_len[0]
    local_keys = jnp.concatenate([local_video[1, 0], own_text[1]], axis=0)
    local_values = jnp.concatenate([local_video[2, 0], own_text[2]], axis=0)
    local_valid = jnp.concatenate([jnp.ones((positions,), bool), own_valid])
    query_scores = (
        jnp.einsum("thd,khd->thk", text_queries, local_keys, preferred_element_type=jnp.float32)
        * score_scale
    )
    query_scores = jnp.where(local_valid, query_scores, masked_score)
    local_max = query_scores.max(-1)
    global_max = lax.pmax(local_max, "frame")
    query_exp = jnp.exp(query_scores - global_max[..., None])
    query_totals = query_exp.sum(-1)
    query_sums = jnp.einsum(
        "thk,khd->thd",
        query_exp.astype(jnp.bfloat16),
        local_values,
        preferred_element_type=jnp.float32,
    )
    query_totals, query_sums = (query_totals, query_sums)
    query_sums, query_totals = (
        lax.psum_scatter(query_sums, "frame", scatter_dimension=0, tiled=True),
        lax.psum_scatter(query_totals, "frame", scatter_dimension=0, tiled=True),
    )
    text_out = (
        (query_sums / query_totals[..., None]).astype(jnp.bfloat16).reshape(shard_text, head_width)
    )
    return (video_out, text_out)


f32 = jnp.float32
bf16 = jnp.bfloat16


def dot_nt(a, b):
    return lax.dot_general(a, b, (((1,), (1,)), ((), ())), preferred_element_type=f32)


def dot_nn(a, b):
    return lax.dot_general(a, b, (((1,), (0,)), ((), ())), preferred_element_type=f32)


def softmax_parts(scores):
    top = scores.max(-1, keepdims=True)
    e = jnp.exp(scores - top)
    return top, e.sum(-1, keepdims=True), e.astype(bf16)


def remote(src, dst, send_sem, recv_sem, peer):
    return pltpu.make_async_remote_copy(
        src_ref=src,
        dst_ref=dst,
        send_sem=send_sem,
        recv_sem=recv_sem,
        device_id={"frame": peer},
        device_id_type=pl.DeviceIdType.MESH,
    )


def kernel(
    n,
    heads,
    kind_ref,
    len_ref,
    video_ref,
    text_ref,
    video_out,
    text_out,
    pair_video,
    pair_text,
    q_all,
    kv_all,
    t_send,
    t_recv,
    o_send,
    o_recv,
    p_send,
    p_recv,
    m_send,
    m_recv,
    result,
    pair_s,
    pair_r,
    q_s,
    q_r,
    kv_s,
    kv_r,
    fw_s,
    t_s,
    t_r,
    o_s,
    o_r,
    p_s,
    p_r,
    m_s,
    m_r,
):
    half = heads // 2
    twins = n // 2
    positions = video_ref.shape[1]
    hd = video_ref.shape[2] // heads
    shard = text_ref.shape[1]
    piece = positions // n
    text_total = n * shard
    rows = twins * shard
    scale = hd ** (-0.5)
    me = lax.axis_index("frame")
    parity = lax.rem(me, 2)
    partner = me + 1 - 2 * parity
    mine = me // 2

    barrier = pltpu.get_barrier_semaphore()

    def greet(k, c):
        pl.semaphore_signal(
            barrier,
            inc=1,
            device_id={"frame": lax.rem(me + k, n)},
            device_id_type=pl.DeviceIdType.MESH,
        )
        return c

    lax.fori_loop(1, n, greet, 0)

    spatial_seen = jnp.int32(0)
    temporal_seen = jnp.int32(0)
    places = []
    for h in range(heads):
        kind = kind_ref[h]
        place = jnp.where(kind == 0, spatial_seen, half + temporal_seen)
        places.append(place)
        spatial_seen = spatial_seen + jnp.where(kind == 0, 1, 0)
        temporal_seen = temporal_seen + jnp.where(kind == 0, 0, 1)

    def in_slot(i, load):
        first = i % half
        block = load(slice(first * hd, (first + 1) * hd))
        for h in range(first + 1, first + half + 1):
            block = jnp.where(places[h] == i, load(slice(h * hd, (h + 1) * hd)), block)
        return block

    for i in range(half):
        for t in range(2):
            kv_all[me, t, :, i * hd : (i + 1) * hd] = in_slot(i, lambda c: text_ref[t + 1, :, c])
    q_all[mine] = text_ref[0]

    for i in range(half):
        for t in range(3):
            whole = in_slot(half + i, lambda c: video_ref[t, :, c])
            whole = whole.astype(f32).reshape(n, piece, hd)
            t_send[:, t, :, i * hd : (i + 1) * hd] = whole.astype(bf16)

    pl.semaphore_wait(barrier, n - 1)

    def pair_copies():
        return (
            remote(video_ref.at[1:3], pair_video, pair_s.at[0], pair_r.at[0], partner),
            remote(text_ref.at[1:3], pair_text, pair_s.at[1], pair_r.at[1], partner),
            remote(kv_all.at[me], kv_all.at[me], fw_s.at[mine], kv_r.at[me], partner),
        )

    for c in pair_copies():
        c.start()

    def twin(k):
        return lax.rem(me + 2 * k, n)

    def q_copy(to):
        return remote(q_all.at[mine], q_all.at[mine], q_s.at[to // 2], q_r.at[mine], to)

    def kv_copy(to):
        return remote(kv_all.at[me], kv_all.at[me], kv_s.at[to // 2], kv_r.at[me], to)

    def t_copy(to):
        return remote(t_send.at[to], t_recv.at[me], t_s.at[to], t_r.at[me], to)

    def landed(dst, sem):
        remote(dst, dst, sem, sem, partner).wait_recv()

    def sent(src, sem):
        remote(src, src, sem, sem, partner).wait_send()

    def start_q(k, c):
        q_copy(twin(k)).start()
        return c

    def start_kv(k, c):
        kv_copy(twin(k)).start()
        return c

    def start_t(k, c):
        t_copy(lax.rem(me + k, n)).start()
        return c

    lax.fori_loop(1, twins, start_q, 0)
    lax.fori_loop(1, n, start_t, 0)
    lax.fori_loop(1, twins, start_kv, 0)
    t_recv[me] = t_send[me]

    landed(pair_video, pair_r.at[0])
    landed(pair_text, pair_r.at[1])

    def wait_q(k, c):
        j = twin(k) // 2
        landed(q_all.at[j], q_r.at[j])
        return c

    lax.fori_loop(1, twins, wait_q, 0)

    length = len_ref[0]
    key = lax.broadcasted_iota(jnp.int32, (1, 2 * positions + 2 * shard), 1)
    offset = key - 2 * positions
    token = jnp.where(offset < shard, me * shard + offset, partner * shard + offset - shard)
    key_ok = (offset < 0) | (token < length)
    lane = lax.broadcasted_iota(jnp.int32, (rows, 128), 1)
    stats = jnp.where(lane < 64, 0.0, 1.0).astype(f32)
    for h in range(heads):
        hs = slice(h * hd, (h + 1) * hd)
        q = q_all[:, :, hs].reshape(rows, hd)
        keys = jnp.concatenate(
            [video_ref[1, :, hs], pair_video[0, :, hs], text_ref[1, :, hs], pair_text[0, :, hs]],
            axis=0,
        )
        values = jnp.concatenate(
            [video_ref[2, :, hs], pair_video[1, :, hs], text_ref[2, :, hs], pair_text[1, :, hs]],
            axis=0,
        )
        s = jnp.where(key_ok, dot_nt(q, keys) * scale, masked_score)
        top, total, w = softmax_parts(s)
        p_send[:, :, hs] = dot_nn(w, values).astype(bf16).reshape(twins, shard, hd)
        stats = jnp.where(lane == h, top, jnp.where(lane == h + 64, total, stats))
    m_send[...] = stats.reshape(twins, shard, 128)

    def p_copy(to):
        return remote(
            p_send.at[to // 2], p_recv.at[mine], p_s.at[to // 2], p_r.at[mine], to
        )

    def m_copy(to):
        return remote(
            m_send.at[to // 2], m_recv.at[mine], m_s.at[to // 2], m_r.at[mine], to
        )

    def start_p(k, c):
        p_copy(twin(k)).start()
        m_copy(twin(k)).start()
        return c

    lax.fori_loop(1, twins, start_p, 0)
    p_recv[mine] = p_send[mine]
    m_recv[mine] = m_send[mine]

    def wait_t(k, c):
        j = lax.rem(me + k, n)
        landed(t_recv.at[j], t_r.at[j])
        return c

    lax.fori_loop(1, n, wait_t, 0)
    count = n * piece
    row_at = lax.rem(lax.broadcasted_iota(jnp.int32, (count, count), 0), piece)
    col_at = lax.rem(lax.broadcasted_iota(jnp.int32, (count, count), 1), piece)
    same = row_at == col_at
    for i in range(half):
        hs = slice(i * hd, (i + 1) * hd)
        q, k_, v = (
            t_recv[:, t, :, hs].astype(f32).reshape(count, hd).astype(bf16) for t in range(3)
        )
        s = jnp.where(same, dot_nt(q, k_) * scale, masked_score)
        top, total, w = softmax_parts(s)
        o = dot_nn(w, v) / total
        o_send[:, :, hs] = o.reshape(n, piece, hd).astype(bf16)

    def o_copy(to):
        return remote(o_send.at[to], o_recv.at[me], o_s.at[to], o_r.at[me], to)

    def start_o(k, c):
        o_copy(lax.rem(me + k, n)).start()
        return c

    lax.fori_loop(1, n, start_o, 0)
    o_recv[me] = o_send[me]

    def fw_copy(j):
        return remote(kv_all.at[j], kv_all.at[j], fw_s.at[j // 2], kv_r.at[j], partner)

    def forward(k, c):
        j = lax.rem(me + n - 2 * k, n)
        landed(kv_all.at[j], kv_r.at[j])
        fw_copy(j).start()
        return c

    lax.fori_loop(1, twins, forward, 0)

    def wait_kv(k, c):
        j = lax.rem(partner + 2 * k, n)
        landed(kv_all.at[j], kv_r.at[j])
        return c

    lax.fori_loop(0, twins, wait_kv, 0)
    text_key = lax.broadcasted_iota(jnp.int32, (1, positions + text_total), 1) - positions
    joint_ok = text_key < length
    for i in range(half):
        q, k_, v = (in_slot(i, lambda c: video_ref[t, :, c]) for t in range(3))
        hs = slice(i * hd, (i + 1) * hd)
        keys = jnp.concatenate(
            [k_, kv_all[:, 0, :, hs].reshape(text_total, hd)], axis=0
        )
        values = jnp.concatenate(
            [v, kv_all[:, 1, :, hs].reshape(text_total, hd)], axis=0
        )
        s = jnp.where(joint_ok, dot_nt(q, keys) * scale, masked_score)
        top, total, w = softmax_parts(s)
        result[i] = (dot_nn(w, values) / total).astype(bf16)

    for h in range(heads):
        block = result[max(0, h - half)]
        for i in range(max(0, h - half) + 1, min(h, half - 1) + 1):
            block = jnp.where(places[h] == i, result[i], block)
        video_out[:, h * hd : (h + 1) * hd] = block

    def wait_p(k, c):
        j = twin(k) // 2
        landed(p_recv.at[j], p_r.at[j])
        landed(m_recv.at[j], m_r.at[j])
        return c

    lax.fori_loop(1, twins, wait_p, 0)
    tops = m_recv[...]
    sums = pltpu.roll(tops.reshape(rows, 128), 64, 1).reshape(twins, shard, 128)
    best = tops.max(0, keepdims=True)
    weight = jnp.exp(jnp.minimum(tops - best, 0.0))
    total = (weight * sums).sum(0)
    for h in range(heads):
        hs = slice(h * hd, (h + 1) * hd)
        merged = (weight[:, :, h : h + 1] * p_recv[:, :, hs].astype(f32)).sum(0)
        text_out[:, hs] = (merged / total[:, h : h + 1]).astype(bf16)

    def wait_o(k, c):
        j = lax.rem(me + k, n)
        landed(o_recv.at[j], o_r.at[j])
        return c

    lax.fori_loop(1, n, wait_o, 0)
    for i in range(half):
        hs = slice(i * hd, (i + 1) * hd)
        result[half + i] = o_recv[:, :, hs].astype(f32).reshape(positions, hd).astype(bf16)
    for h in range(heads):
        hs = slice(h * hd, (h + 1) * hd)
        block = video_out[:, hs]
        for i in range(max(0, h - half), min(h, half - 1) + 1):
            block = jnp.where(places[h] == half + i, result[half + i], block)
        video_out[:, hs] = block

    sent(pair_video, pair_s.at[0])
    sent(pair_text, pair_s.at[1])
    sent(kv_all.at[me], fw_s.at[mine])

    def drain_twin(k, c):
        j = twin(k) // 2
        sent(q_all.at[j], q_s.at[j])
        sent(kv_all.at[me], kv_s.at[j])
        sent(kv_all.at[me], fw_s.at[j])
        sent(p_send.at[j], p_s.at[j])
        sent(m_send.at[j], m_s.at[j])
        return c

    lax.fori_loop(1, twins, drain_twin, 0)

    def drain_all(k, c):
        j = lax.rem(me + k, n)
        sent(t_send.at[j], t_s.at[j])
        sent(o_send.at[j], o_s.at[j])
        return c

    lax.fori_loop(1, n, drain_all, 0)


def fused_body(n, video_qkv, text_qkv, head_kind, text_len):
    heads = head_kind.shape[0]
    _, _, positions, width = video_qkv.shape
    shard = text_qkv.shape[1]
    half, twins, piece = heads // 2, n // 2, positions // n
    hd = width // heads
    narrow = half * hd
    vmem = pl.BlockSpec(memory_space=pltpu.VMEM)
    smem = pl.BlockSpec(memory_space=pltpu.SMEM)
    dma = pltpu.SemaphoreType.DMA
    video_out, text_out = pl.pallas_call(
        functools.partial(kernel, n, heads),
        out_shape=(
            jax.ShapeDtypeStruct((positions, width), bf16),
            jax.ShapeDtypeStruct((shard, width), bf16),
        ),
        in_specs=[smem, smem, vmem, vmem],
        out_specs=(vmem, vmem),
        scratch_shapes=[
            pltpu.VMEM((2, positions, width), bf16),
            pltpu.VMEM((2, shard, width), bf16),
            pltpu.VMEM((twins, shard, width), bf16),
            pltpu.VMEM((n, 2, shard, narrow), bf16),
            pltpu.VMEM((n, 3, piece, narrow), bf16),
            pltpu.VMEM((n, 3, piece, narrow), bf16),
            pltpu.VMEM((n, piece, narrow), bf16),
            pltpu.VMEM((n, piece, narrow), bf16),
            pltpu.VMEM((twins, shard, width), bf16),
            pltpu.VMEM((twins, shard, width), bf16),
            pltpu.VMEM((twins, shard, 128), f32),
            pltpu.VMEM((twins, shard, 128), f32),
            pltpu.VMEM((heads, positions, hd), bf16),
            dma((2,)),
            dma((2,)),
            dma((twins,)),
            dma((twins,)),
            dma((twins,)),
            dma((n,)),
            dma((twins,)),
            dma((n,)),
            dma((n,)),
            dma((n,)),
            dma((n,)),
            dma((twins,)),
            dma((twins,)),
            dma((twins,)),
            dma((twins,)),
        ],
        compiler_params=pltpu.CompilerParams(
            collective_id=0, has_side_effects=True, vmem_limit_bytes=40 << 20
        ),
    )(head_kind, text_len, video_qkv.reshape(3, positions, width), text_qkv)
    return video_out.reshape(1, positions, width), text_out


def body(n, video_qkv, text_qkv, head_kind, text_len):
    heads = head_kind.shape[0]
    positions, width = video_qkv.shape[2:]
    shard = text_qkv.shape[1]
    whole_tiles = (
        video_qkv.shape[1] == 1
        and n % 2 == 0
        and heads % 2 == 0
        and heads <= 64
        and shard % 16 == 0
        and positions % (8 * n) == 0
        and (width // heads) % 128 == 0
    )
    if whole_tiles:
        return fused_body(n, video_qkv, text_qkv, head_kind, text_len)
    return plain_body(video_qkv, text_qkv, head_kind, text_len)


def solution(mesh):
    in_specs = (
        P(None, ("groups", "frame"), None, None),
        P(None, ("groups", "frame"), None),
        P("groups"),
        P("groups"),
    )
    out_specs = (P(("groups", "frame"), None, None), P(("groups", "frame"), None))
    return jax.shard_map(
        functools.partial(body, mesh.shape["frame"]), mesh=mesh, in_specs=in_specs, out_specs=out_specs, check_vma=False)
```

```python
import functools

import jax
import jax.numpy as jnp
from jax import lax
from jax.experimental import pallas as pl
from jax.experimental.pallas import tpu as pltpu
from jax.sharding import PartitionSpec as P

masked_score = -1e30


def plain_body(video_qkv, text_qkv, head_kind, text_len):
    head_count = head_kind.shape[0]
    head_width = video_qkv.shape[-1]
    head_dim = head_width // head_count
    positions = video_qkv.shape[2]
    shard_text = text_qkv.shape[1]
    score_scale = head_dim ** (-0.5)
    device_rank = lax.axis_index("frame")
    local_video = video_qkv.reshape(3, 1, positions, head_count, head_dim)
    gathered = lax.all_gather(text_qkv, "frame", axis=1, tiled=True)
    text_total = gathered.shape[1]
    all_text = gathered.reshape(3, text_total, head_count, head_dim)
    text_valid = jnp.arange(text_total) < text_len[0]
    spatial_heads = jnp.nonzero(head_kind == 0, size=head_count - head_count // 2)[0].astype(
        jnp.int32
    )
    temporal_heads = jnp.nonzero(head_kind == 1, size=head_count // 2)[0].astype(jnp.int32)
    own_frame = jnp.take(local_video[:, 0], spatial_heads, axis=2)
    text_spatial = jnp.take(all_text[1:], spatial_heads, axis=2)
    joint_keys = jnp.concatenate([own_frame[1], text_spatial[0]], axis=0)
    joint_values = jnp.concatenate([own_frame[2], text_spatial[1]], axis=0)
    joint_valid = jnp.concatenate([jnp.ones((positions,), bool), text_valid])
    spatial_scores = (
        jnp.einsum("phd,khd->hpk", own_frame[0], joint_keys, preferred_element_type=jnp.float32)
        * score_scale
    )
    spatial_scores = jnp.where(joint_valid, spatial_scores, masked_score)
    row_max = spatial_scores.max(-1, keepdims=True)
    spatial_exp = jnp.exp(spatial_scores - row_max)
    totals = spatial_exp.sum(-1)
    summed = jnp.einsum(
        "hpk,khd->phd",
        spatial_exp.astype(jnp.bfloat16),
        joint_values,
        preferred_element_type=jnp.float32,
    )
    spatial_result = (summed / totals.T[..., None]).astype(jnp.bfloat16)
    selected = jnp.take(local_video, temporal_heads, axis=3)
    block = lax.all_to_all(selected, "frame", split_axis=2, concat_axis=1, tiled=True)
    scores = (
        jnp.einsum("fphd,gphd->phfg", block[0], block[1], preferred_element_type=jnp.float32)
        * score_scale
    )
    block_max = scores.max(-1, keepdims=True)
    exps = jnp.exp(scores - block_max)
    block_totals = exps.sum(-1)
    block_sum = jnp.einsum(
        "phfg,gphd->fphd", exps.astype(jnp.bfloat16), block[2], preferred_element_type=jnp.float32
    )
    result = (block_sum / jnp.transpose(block_totals, (2, 0, 1))[..., None]).astype(jnp.bfloat16)
    temporal_result = lax.all_to_all(result, "frame", split_axis=0, concat_axis=1, tiled=True)[0]
    joined = jnp.concatenate([spatial_result, temporal_result], axis=1)
    order = jnp.concatenate([spatial_heads, temporal_heads])
    inverse = jnp.argsort(order)
    video_out = jnp.take(joined, inverse, axis=1).reshape(1, positions, head_width)
    text_queries = all_text[0]
    own_text = text_qkv.reshape(3, shard_text, head_count, head_dim)
    own_valid = device_rank * shard_text + jnp.arange(shard_text) < text_len[0]
    local_keys = jnp.concatenate([local_video[1, 0], own_text[1]], axis=0)
    local_values = jnp.concatenate([local_video[2, 0], own_text[2]], axis=0)
    local_valid = jnp.concatenate([jnp.ones((positions,), bool), own_valid])
    query_scores = (
        jnp.einsum("thd,khd->thk", text_queries, local_keys, preferred_element_type=jnp.float32)
        * score_scale
    )
    query_scores = jnp.where(local_valid, query_scores, masked_score)
    local_max = query_scores.max(-1)
    global_max = lax.pmax(local_max, "frame")
    query_exp = jnp.exp(query_scores - global_max[..., None])
    query_totals = query_exp.sum(-1)
    query_sums = jnp.einsum(
        "thk,khd->thd",
        query_exp.astype(jnp.bfloat16),
        local_values,
        preferred_element_type=jnp.float32,
    )
    query_totals, query_sums = (query_totals, query_sums)
    query_sums, query_totals = (
        lax.psum_scatter(query_sums, "frame", scatter_dimension=0, tiled=True),
        lax.psum_scatter(query_totals, "frame", scatter_dimension=0, tiled=True),
    )
    text_out = (
        (query_sums / query_totals[..., None]).astype(jnp.bfloat16).reshape(shard_text, head_width)
    )
    return (video_out, text_out)


f32 = jnp.float32
bf16 = jnp.bfloat16


def dot_nt(a, b):
    return lax.dot_general(a, b, (((1,), (1,)), ((), ())), preferred_element_type=f32)


def dot_nn(a, b):
    return lax.dot_general(a, b, (((1,), (0,)), ((), ())), preferred_element_type=f32)


def softmax_parts(scores):
    top = scores.max(-1, keepdims=True)
    e = jnp.exp(scores - top)
    return top, e.sum(-1, keepdims=True), e.astype(bf16)


def remote(src, dst, send_sem, recv_sem, peer):
    return pltpu.make_async_remote_copy(
        src_ref=src,
        dst_ref=dst,
        send_sem=send_sem,
        recv_sem=recv_sem,
        device_id={"frame": peer},
        device_id_type=pl.DeviceIdType.MESH,
    )


def kernel(
    n,
    heads,
    kind_hbm,
    len_hbm,
    video_hbm,
    text_hbm,
    video_out,
    text_out,
    kind_ref,
    len_ref,
    video_ref,
    text_ref,
    pair_video,
    pair_text,
    q_all,
    kv_all,
    t_send,
    t_recv,
    o_send,
    o_recv,
    p_send,
    p_recv,
    m_send,
    m_recv,
    result,
    in_sem,
    pair_s,
    pair_r,
    q_s,
    qf_s,
    q_r,
    kv_s,
    kv_r,
    fw_s,
    fy_s,
    t_s,
    t_r,
    o_s,
    o_r,
    p_s,
    p_r,
    m_s,
    m_r,
):
    half = heads // 2
    twins = n // 2
    positions = video_ref.shape[1]
    hd = video_ref.shape[2] // heads
    shard = text_ref.shape[1]
    piece = positions // n
    text_total = n * shard
    rows = twins * shard
    scale = hd ** (-0.5)
    me = lax.axis_index("frame")
    parity = lax.rem(me, 2)
    across = me + 2 - 4 * lax.rem(me // 2, 2)
    row_count = n // 4
    partner = me + 1 - 2 * parity
    mine = me // 2

    barrier = pltpu.get_barrier_semaphore()

    def greet(k, c):
        pl.semaphore_signal(
            barrier,
            inc=1,
            device_id={"frame": lax.rem(me + k, n)},
            device_id_type=pl.DeviceIdType.MESH,
        )
        return c

    inputs = [
        pltpu.make_async_copy(a, b, in_sem.at[i])
        for i, (a, b) in enumerate(
            (
                (kind_hbm, kind_ref),
                (len_hbm, len_ref),
                (text_hbm, text_ref),
                (video_hbm, video_ref),
            )
        )
    ]
    for copy in inputs:
        copy.start()
    lax.fori_loop(1, n, greet, 0)
    for copy in inputs:
        copy.wait()

    spatial_seen = jnp.int32(0)
    temporal_seen = jnp.int32(0)
    places = []
    for h in range(heads):
        kind = kind_ref[h]
        place = jnp.where(kind == 0, spatial_seen, half + temporal_seen)
        places.append(place)
        spatial_seen = spatial_seen + jnp.where(kind == 0, 1, 0)
        temporal_seen = temporal_seen + jnp.where(kind == 0, 0, 1)

    def in_slot(i, load):
        first = i % half
        block = load(slice(first * hd, (first + 1) * hd))
        for h in range(first + 1, first + half + 1):
            block = jnp.where(places[h] == i, load(slice(h * hd, (h + 1) * hd)), block)
        return block

    for i in range(half):
        for t in range(2):
            kv_all[me, t, :, i * hd : (i + 1) * hd] = in_slot(i, lambda c: text_ref[t + 1, :, c])
    q_all[mine] = text_ref[0]

    for i in range(half):
        for t in range(3):
            whole = in_slot(half + i, lambda c: video_ref[t, :, c])
            whole = whole.astype(f32).reshape(n, piece, hd)
            t_send[:, t, :, i * hd : (i + 1) * hd] = whole.astype(bf16)

    pl.semaphore_wait(barrier, n - 1)

    def pair_copies():
        return (
            remote(video_hbm.at[1:3], pair_video, pair_s.at[0], pair_r.at[0], partner),
            remote(text_hbm.at[1:3], pair_text, pair_s.at[1], pair_r.at[1], partner),
            remote(kv_all.at[me], kv_all.at[me], fw_s.at[mine], kv_r.at[me], partner),
        )

    for c in pair_copies():
        c.start()

    def twin(k):
        return lax.rem(me + 2 * k, n)

    def q_copy(to):
        return remote(q_all.at[mine], q_all.at[mine], q_s.at[to // 2], q_r.at[mine], to)

    def kv_copy(to):
        return remote(kv_all.at[me], kv_all.at[me], kv_s.at[to // 2], kv_r.at[me], to)

    def t_copy(to):
        return remote(t_send.at[to], t_recv.at[me], t_s.at[to], t_r.at[me], to)

    def landed(dst, sem):
        remote(dst, dst, sem, sem, partner).wait_recv()

    def sent(src, sem):
        remote(src, src, sem, sem, partner).wait_send()

    def start_t(k, c):
        t_copy(lax.rem(me + k, n)).start()
        return c

    def along(k):
        return lax.rem(me + 4 * k, n)

    def back(k):
        return lax.rem(me + n - 4 * k, n)

    def start_text(k, c):
        q_copy(along(k)).start()
        kv_copy(along(k)).start()
        return c

    q_copy(across).start()
    lax.fori_loop(1, row_count, start_text, 0)
    kv_copy(across).start()
    lax.fori_loop(1, n, start_t, 0)
    t_recv[me] = t_send[me]

    def qf_copy(j):
        return remote(q_all.at[j // 2], q_all.at[j // 2], qf_s.at[j // 2], q_r.at[j // 2], across)

    def fw_copy(j):
        return remote(kv_all.at[j], kv_all.at[j], fw_s.at[j // 2], kv_r.at[j], partner)

    def fy_copy(j):
        return remote(kv_all.at[j], kv_all.at[j], fy_s.at[j // 2], kv_r.at[j], across)

    def forward_text(k, c):
        j = back(k)
        landed(q_all.at[j // 2], q_r.at[j // 2])
        qf_copy(j).start()
        landed(kv_all.at[j], kv_r.at[j])
        fy_copy(j).start()
        fw_copy(j).start()
        return c

    lax.fori_loop(1, row_count, forward_text, 0)

    landed(pair_video, pair_r.at[0])
    landed(pair_text, pair_r.at[1])

    def wait_q(k, c):
        j = lax.rem(across + n - 4 * k, n) // 2
        landed(q_all.at[j], q_r.at[j])
        return c

    lax.fori_loop(0, row_count, wait_q, 0)

    length = len_ref[0]
    key = lax.broadcasted_iota(jnp.int32, (1, 2 * positions + 2 * shard), 1)
    offset = key - 2 * positions
    token = jnp.where(offset < shard, me * shard + offset, partner * shard + offset - shard)
    key_ok = (offset < 0) | (token < length)
    lane = lax.broadcasted_iota(jnp.int32, (rows, 128), 1)
    stats = jnp.where(lane < 64, 0.0, 1.0).astype(f32)
    for h in range(heads):
        hs = slice(h * hd, (h + 1) * hd)
        q = q_all[:, :, hs].reshape(rows, hd)
        keys = jnp.concatenate(
            [video_ref[1, :, hs], pair_video[0, :, hs], text_ref[1, :, hs], pair_text[0, :, hs]],
            axis=0,
        )
        values = jnp.concatenate(
            [video_ref[2, :, hs], pair_video[1, :, hs], text_ref[2, :, hs], pair_text[1, :, hs]],
            axis=0,
        )
        s = jnp.where(key_ok, dot_nt(q, keys) * scale, masked_score)
        top, total, w = softmax_parts(s)
        p_send[:, :, hs] = dot_nn(w, values).astype(bf16).reshape(twins, shard, hd)
        stats = jnp.where(lane == h, top, jnp.where(lane == h + 64, total, stats))
    m_send[...] = stats.reshape(twins, shard, 128)

    def p_copy(to):
        return remote(
            p_send.at[to // 2], p_recv.at[mine], p_s.at[to // 2], p_r.at[mine], to
        )

    def m_copy(to):
        return remote(
            m_send.at[to // 2], m_recv.at[mine], m_s.at[to // 2], m_r.at[mine], to
        )

    def start_p(k, c):
        p_copy(twin(k)).start()
        m_copy(twin(k)).start()
        return c

    lax.fori_loop(1, twins, start_p, 0)
    p_recv[mine] = p_send[mine]
    m_recv[mine] = m_send[mine]

    def wait_t(k, c):
        j = lax.rem(me + k, n)
        landed(t_recv.at[j], t_r.at[j])
        return c

    lax.fori_loop(1, n, wait_t, 0)
    count = n * piece
    row_at = lax.rem(lax.broadcasted_iota(jnp.int32, (count, count), 0), piece)
    col_at = lax.rem(lax.broadcasted_iota(jnp.int32, (count, count), 1), piece)
    same = row_at == col_at
    for i in range(half):
        hs = slice(i * hd, (i + 1) * hd)
        q, k_, v = (
            t_recv[:, t, :, hs].astype(f32).reshape(count, hd).astype(bf16) for t in range(3)
        )
        s = jnp.where(same, dot_nt(q, k_) * scale, masked_score)
        top, total, w = softmax_parts(s)
        o = dot_nn(w, v) / total
        o_send[:, :, hs] = o.reshape(n, piece, hd).astype(bf16)

    def o_copy(to):
        return remote(o_send.at[to], o_recv.at[me], o_s.at[to], o_r.at[me], to)

    def start_o(k, c):
        o_copy(lax.rem(me + k, n)).start()
        return c

    lax.fori_loop(1, n, start_o, 0)
    o_recv[me] = o_send[me]

    def forward(k, c):
        j = lax.rem(across + n - 4 * k, n)
        landed(kv_all.at[j], kv_r.at[j])
        fw_copy(j).start()
        return c

    lax.fori_loop(0, row_count, forward, 0)

    def wait_kv(k, c):
        j = lax.rem(partner + 2 * k, n)
        landed(kv_all.at[j], kv_r.at[j])
        return c

    lax.fori_loop(0, twins, wait_kv, 0)
    text_key = lax.broadcasted_iota(jnp.int32, (1, positions + text_total), 1) - positions
    joint_ok = text_key < length
    for i in range(half):
        q, k_, v = (in_slot(i, lambda c: video_ref[t, :, c]) for t in range(3))
        hs = slice(i * hd, (i + 1) * hd)
        keys = jnp.concatenate(
            [k_, kv_all[:, 0, :, hs].reshape(text_total, hd)], axis=0
        )
        values = jnp.concatenate(
            [v, kv_all[:, 1, :, hs].reshape(text_total, hd)], axis=0
        )
        s = jnp.where(joint_ok, dot_nt(q, keys) * scale, masked_score)
        top, total, w = softmax_parts(s)
        result[i] = (dot_nn(w, values) / total).astype(bf16)

    for h in range(heads):
        block = result[max(0, h - half)]
        for i in range(max(0, h - half) + 1, min(h, half - 1) + 1):
            block = jnp.where(places[h] == i, result[i], block)
        video_out[:, h * hd : (h + 1) * hd] = block

    def wait_p(k, c):
        j = twin(k) // 2
        landed(p_recv.at[j], p_r.at[j])
        landed(m_recv.at[j], m_r.at[j])
        return c

    lax.fori_loop(1, twins, wait_p, 0)
    tops = m_recv[...]
    sums = pltpu.roll(tops.reshape(rows, 128), 64, 1).reshape(twins, shard, 128)
    best = tops.max(0, keepdims=True)
    weight = jnp.exp(jnp.minimum(tops - best, 0.0))
    total = (weight * sums).sum(0)
    for h in range(heads):
        hs = slice(h * hd, (h + 1) * hd)
        merged = (weight[:, :, h : h + 1] * p_recv[:, :, hs].astype(f32)).sum(0)
        text_out[:, hs] = (merged / total[:, h : h + 1]).astype(bf16)

    def wait_o(k, c):
        j = lax.rem(me + k, n)
        landed(o_recv.at[j], o_r.at[j])
        return c

    lax.fori_loop(1, n, wait_o, 0)
    for i in range(half):
        hs = slice(i * hd, (i + 1) * hd)
        result[half + i] = o_recv[:, :, hs].astype(f32).reshape(positions, hd).astype(bf16)
    for h in range(heads):
        hs = slice(h * hd, (h + 1) * hd)
        block = video_out[:, hs]
        for i in range(max(0, h - half), min(h, half - 1) + 1):
            block = jnp.where(places[h] == half + i, result[half + i], block)
        video_out[:, hs] = block

    sent(pair_video, pair_s.at[0])
    sent(pair_text, pair_s.at[1])
    sent(kv_all.at[me], fw_s.at[mine])

    sent(q_all.at[mine], q_s.at[across // 2])
    sent(kv_all.at[me], kv_s.at[across // 2])

    def drain_row(k, c):
        j = along(k) // 2
        sent(q_all.at[j], q_s.at[j])
        sent(kv_all.at[me], kv_s.at[j])
        sent(q_all.at[j], qf_s.at[j])
        sent(kv_all.at[me], fy_s.at[j])
        return c

    lax.fori_loop(1, row_count, drain_row, 0)

    def drain_twin(k, c):
        j = twin(k) // 2
        sent(kv_all.at[me], fw_s.at[j])
        sent(p_send.at[j], p_s.at[j])
        sent(m_send.at[j], m_s.at[j])
        return c

    lax.fori_loop(1, twins, drain_twin, 0)

    def drain_all(k, c):
        j = lax.rem(me + k, n)
        sent(t_send.at[j], t_s.at[j])
        sent(o_send.at[j], o_s.at[j])
        return c

    lax.fori_loop(1, n, drain_all, 0)


def fused_body(n, video_qkv, text_qkv, head_kind, text_len):
    heads = head_kind.shape[0]
    _, _, positions, width = video_qkv.shape
    shard = text_qkv.shape[1]
    half, twins, piece = heads // 2, n // 2, positions // n
    hd = width // heads
    narrow = half * hd
    vmem = pl.BlockSpec(memory_space=pltpu.VMEM)
    hbm = pl.BlockSpec(memory_space=pltpu.HBM)
    dma = pltpu.SemaphoreType.DMA
    video_out, text_out = pl.pallas_call(
        functools.partial(kernel, n, heads),
        out_shape=(
            jax.ShapeDtypeStruct((positions, width), bf16),
            jax.ShapeDtypeStruct((shard, width), bf16),
        ),
        in_specs=[hbm] * 4,
        out_specs=(vmem, vmem),
        scratch_shapes=[
            pltpu.SMEM((heads,), jnp.int32),
            pltpu.SMEM((1,), jnp.int32),
            pltpu.VMEM((3, positions, width), bf16),
            pltpu.VMEM((3, shard, width), bf16),
            pltpu.VMEM((2, positions, width), bf16),
            pltpu.VMEM((2, shard, width), bf16),
            pltpu.VMEM((twins, shard, width), bf16),
            pltpu.VMEM((n, 2, shard, narrow), bf16),
            pltpu.VMEM((n, 3, piece, narrow), bf16),
            pltpu.VMEM((n, 3, piece, narrow), bf16),
            pltpu.VMEM((n, piece, narrow), bf16),
            pltpu.VMEM((n, piece, narrow), bf16),
            pltpu.VMEM((twins, shard, width), bf16),
            pltpu.VMEM((twins, shard, width), bf16),
            pltpu.VMEM((twins, shard, 128), f32),
            pltpu.VMEM((twins, shard, 128), f32),
            pltpu.VMEM((heads, positions, hd), bf16),
            dma((4,)),
            dma((2,)),
            dma((2,)),
            dma((twins,)),
            dma((twins,)),
            dma((twins,)),
            dma((twins,)),
            dma((n,)),
            dma((twins,)),
            dma((twins,)),
            dma((n,)),
            dma((n,)),
            dma((n,)),
            dma((n,)),
            dma((twins,)),
            dma((twins,)),
            dma((twins,)),
            dma((twins,)),
        ],
        compiler_params=pltpu.CompilerParams(
            collective_id=0, has_side_effects=True, vmem_limit_bytes=63 << 20
        ),
    )(head_kind, text_len, video_qkv.reshape(3, positions, width), text_qkv)
    return video_out.reshape(1, positions, width), text_out


def body(n, video_qkv, text_qkv, head_kind, text_len):
    heads = head_kind.shape[0]
    positions, width = video_qkv.shape[2:]
    shard = text_qkv.shape[1]
    whole_tiles = (
        video_qkv.shape[1] == 1
        and n % 4 == 0
        and heads % 2 == 0
        and heads <= 64
        and shard % 16 == 0
        and positions % (8 * n) == 0
        and (width // heads) % 128 == 0
    )
    if whole_tiles:
        return fused_body(n, video_qkv, text_qkv, head_kind, text_len)
    return plain_body(video_qkv, text_qkv, head_kind, text_len)


def solution(mesh):
    in_specs = (
        P(None, ("groups", "frame"), None, None),
        P(None, ("groups", "frame"), None),
        P("groups"),
        P("groups"),
    )
    out_specs = (P(("groups", "frame"), None, None), P(("groups", "frame"), None))
    return jax.shard_map(
        functools.partial(body, mesh.shape["frame"]), mesh=mesh, in_specs=in_specs, out_specs=out_specs, check_vma=False)
```

```python
import functools

import jax
import jax.numpy as jnp
from jax import lax
from jax.experimental import pallas as pl
from jax.experimental.pallas import tpu as pltpu
from jax.sharding import PartitionSpec as P

masked_score = -1e30


def plain_body(video_qkv, text_qkv, head_kind, text_len):
    head_count = head_kind.shape[0]
    head_width = video_qkv.shape[-1]
    head_dim = head_width // head_count
    positions = video_qkv.shape[2]
    shard_text = text_qkv.shape[1]
    score_scale = head_dim ** (-0.5)
    device_rank = lax.axis_index("frame")
    local_video = video_qkv.reshape(3, 1, positions, head_count, head_dim)
    gathered = lax.all_gather(text_qkv, "frame", axis=1, tiled=True)
    text_total = gathered.shape[1]
    all_text = gathered.reshape(3, text_total, head_count, head_dim)
    text_valid = jnp.arange(text_total) < text_len[0]
    spatial_heads = jnp.nonzero(head_kind == 0, size=head_count - head_count // 2)[0].astype(
        jnp.int32
    )
    temporal_heads = jnp.nonzero(head_kind == 1, size=head_count // 2)[0].astype(jnp.int32)
    own_frame = jnp.take(local_video[:, 0], spatial_heads, axis=2)
    text_spatial = jnp.take(all_text[1:], spatial_heads, axis=2)
    joint_keys = jnp.concatenate([own_frame[1], text_spatial[0]], axis=0)
    joint_values = jnp.concatenate([own_frame[2], text_spatial[1]], axis=0)
    joint_valid = jnp.concatenate([jnp.ones((positions,), bool), text_valid])
    spatial_scores = (
        jnp.einsum("phd,khd->hpk", own_frame[0], joint_keys, preferred_element_type=jnp.float32)
        * score_scale
    )
    spatial_scores = jnp.where(joint_valid, spatial_scores, masked_score)
    row_max = spatial_scores.max(-1, keepdims=True)
    spatial_exp = jnp.exp(spatial_scores - row_max)
    totals = spatial_exp.sum(-1)
    summed = jnp.einsum(
        "hpk,khd->phd",
        spatial_exp.astype(jnp.bfloat16),
        joint_values,
        preferred_element_type=jnp.float32,
    )
    spatial_result = (summed / totals.T[..., None]).astype(jnp.bfloat16)
    selected = jnp.take(local_video, temporal_heads, axis=3)
    block = lax.all_to_all(selected, "frame", split_axis=2, concat_axis=1, tiled=True)
    scores = (
        jnp.einsum("fphd,gphd->phfg", block[0], block[1], preferred_element_type=jnp.float32)
        * score_scale
    )
    block_max = scores.max(-1, keepdims=True)
    exps = jnp.exp(scores - block_max)
    block_totals = exps.sum(-1)
    block_sum = jnp.einsum(
        "phfg,gphd->fphd", exps.astype(jnp.bfloat16), block[2], preferred_element_type=jnp.float32
    )
    result = (block_sum / jnp.transpose(block_totals, (2, 0, 1))[..., None]).astype(jnp.bfloat16)
    temporal_result = lax.all_to_all(result, "frame", split_axis=0, concat_axis=1, tiled=True)[0]
    joined = jnp.concatenate([spatial_result, temporal_result], axis=1)
    order = jnp.concatenate([spatial_heads, temporal_heads])
    inverse = jnp.argsort(order)
    video_out = jnp.take(joined, inverse, axis=1).reshape(1, positions, head_width)
    text_queries = all_text[0]
    own_text = text_qkv.reshape(3, shard_text, head_count, head_dim)
    own_valid = device_rank * shard_text + jnp.arange(shard_text) < text_len[0]
    local_keys = jnp.concatenate([local_video[1, 0], own_text[1]], axis=0)
    local_values = jnp.concatenate([local_video[2, 0], own_text[2]], axis=0)
    local_valid = jnp.concatenate([jnp.ones((positions,), bool), own_valid])
    query_scores = (
        jnp.einsum("thd,khd->thk", text_queries, local_keys, preferred_element_type=jnp.float32)
        * score_scale
    )
    query_scores = jnp.where(local_valid, query_scores, masked_score)
    local_max = query_scores.max(-1)
    global_max = lax.pmax(local_max, "frame")
    query_exp = jnp.exp(query_scores - global_max[..., None])
    query_totals = query_exp.sum(-1)
    query_sums = jnp.einsum(
        "thk,khd->thd",
        query_exp.astype(jnp.bfloat16),
        local_values,
        preferred_element_type=jnp.float32,
    )
    query_totals, query_sums = (query_totals, query_sums)
    query_sums, query_totals = (
        lax.psum_scatter(query_sums, "frame", scatter_dimension=0, tiled=True),
        lax.psum_scatter(query_totals, "frame", scatter_dimension=0, tiled=True),
    )
    text_out = (
        (query_sums / query_totals[..., None]).astype(jnp.bfloat16).reshape(shard_text, head_width)
    )
    return (video_out, text_out)


f32 = jnp.float32
bf16 = jnp.bfloat16


def dot_nt(a, b):
    return lax.dot_general(a, b, (((1,), (1,)), ((), ())), preferred_element_type=f32)


def dot_nn(a, b):
    return lax.dot_general(a, b, (((1,), (0,)), ((), ())), preferred_element_type=f32)


def softmax_parts(scores):
    top = scores.max(-1, keepdims=True)
    e = jnp.exp(scores - top)
    return top, e.sum(-1, keepdims=True), e.astype(bf16)


def remote(src, dst, send_sem, recv_sem, peer):
    return pltpu.make_async_remote_copy(
        src_ref=src,
        dst_ref=dst,
        send_sem=send_sem,
        recv_sem=recv_sem,
        device_id={"frame": peer},
        device_id_type=pl.DeviceIdType.MESH,
    )


def kernel(
    n,
    heads,
    kind_hbm,
    len_hbm,
    video_hbm,
    text_hbm,
    video_out,
    text_out,
    kind_ref,
    len_ref,
    video_ref,
    text_ref,
    pair_video,
    pair_text,
    q_all,
    kv_all,
    t_send,
    t_recv,
    o_send,
    o_recv,
    p_send,
    p_mid,
    p_out,
    p_recv,
    m_send,
    m_mid,
    m_out,
    m_recv,
    result,
    in_sem,
    pair_s,
    pair_r,
    up_s,
    down_s,
    side_s,
    q_r,
    kv_r,
    fw_s,
    t_s,
    t_r,
    o_s,
    o_r,
    pa_s,
    pa_r,
    p_s,
    p_r,
    m_s,
    m_r,
):
    half = heads // 2
    twins = n // 2
    positions = video_ref.shape[1]
    hd = video_ref.shape[2] // heads
    shard = text_ref.shape[1]
    piece = positions // n
    text_total = n * shard
    rows = twins * shard
    scale = hd ** (-0.5)
    me = lax.axis_index("frame")
    parity = lax.rem(me, 2)
    across = me + 2 - 4 * lax.rem(me // 2, 2)
    row_count = n // 4
    partner = me + 1 - 2 * parity
    mine = me // 2

    barrier = pltpu.get_barrier_semaphore()

    def greet(k, c):
        pl.semaphore_signal(
            barrier,
            inc=1,
            device_id={"frame": lax.rem(me + k, n)},
            device_id_type=pl.DeviceIdType.MESH,
        )
        return c

    inputs = [
        pltpu.make_async_copy(a, b, in_sem.at[i])
        for i, (a, b) in enumerate(
            (
                (kind_hbm, kind_ref),
                (len_hbm, len_ref),
                (text_hbm, text_ref),
                (video_hbm, video_ref),
            )
        )
    ]
    for copy in inputs:
        copy.start()
    lax.fori_loop(1, n, greet, 0)
    for copy in inputs:
        copy.wait()

    spatial_seen = jnp.int32(0)
    temporal_seen = jnp.int32(0)
    places = []
    for h in range(heads):
        kind = kind_ref[h]
        place = jnp.where(kind == 0, spatial_seen, half + temporal_seen)
        places.append(place)
        spatial_seen = spatial_seen + jnp.where(kind == 0, 1, 0)
        temporal_seen = temporal_seen + jnp.where(kind == 0, 0, 1)

    def in_slot(i, load):
        first = i % half
        block = load(slice(first * hd, (first + 1) * hd))
        for h in range(first + 1, first + half + 1):
            block = jnp.where(places[h] == i, load(slice(h * hd, (h + 1) * hd)), block)
        return block

    for i in range(half):
        for t in range(2):
            kv_all[me, t, :, i * hd : (i + 1) * hd] = in_slot(i, lambda c: text_ref[t + 1, :, c])
    q_all[mine] = text_ref[0]

    for i in range(half):
        for t in range(3):
            whole = in_slot(half + i, lambda c: video_ref[t, :, c])
            whole = whole.astype(f32).reshape(n, piece, hd)
            t_send[:, t, :, i * hd : (i + 1) * hd] = whole.astype(bf16)

    pl.semaphore_wait(barrier, n - 1)

    def pair_copies():
        return (
            remote(video_hbm.at[1:3], pair_video, pair_s.at[0], pair_r.at[0], partner),
            remote(text_hbm.at[1:3], pair_text, pair_s.at[1], pair_r.at[1], partner),
            remote(kv_all.at[me], kv_all.at[me], fw_s.at[mine], kv_r.at[me], partner),
        )

    for c in pair_copies():
        c.start()

    def along(k):
        return lax.rem(me + 4 * k, n)

    def t_copy(to):
        return remote(t_send.at[to], t_recv.at[me], t_s.at[to], t_r.at[me], to)

    def landed(dst, sem):
        remote(dst, dst, sem, sem, partner).wait_recv()

    def sent(src, sem):
        remote(src, src, sem, sem, partner).wait_send()

    def start_t(k, c):
        t_copy(lax.rem(me + k, n)).start()
        return c

    row = me // 4
    after, before = me + 4, me - 4

    def hop(j, to, sems):
        d = j // 2
        return (
            remote(q_all.at[d], q_all.at[d], sems.at[0, j // 4], q_r.at[d], to),
            remote(kv_all.at[j], kv_all.at[j], sems.at[1, j // 4], kv_r.at[j], to),
        )

    def fw_copy(j):
        return remote(kv_all.at[j], kv_all.at[j], fw_s.at[j // 2], kv_r.at[j], partner)

    def hop_on(j, to, sems):
        for copy in hop(j, to, sems):
            copy.start()

    @pl.when(row < row_count - 1)
    def _():
        hop_on(me, after, up_s)

    @pl.when(row > 0)
    def _():
        hop_on(me, before, down_s)

    hop_on(me, across, side_s)
    lax.fori_loop(1, n, start_t, 0)
    t_recv[me] = t_send[me]

    def arrive(j):
        landed(q_all.at[j // 2], q_r.at[j // 2])
        landed(kv_all.at[j], kv_r.at[j])

    for k in range(1, row_count):

        @pl.when(row >= k)
        def _():
            j = me - 4 * k
            arrive(j)

            @pl.when(row < row_count - 1)
            def _():
                hop_on(j, after, up_s)

            hop_on(j, across, side_s)
            fw_copy(j).start()

        @pl.when(row + k < row_count)
        def _():
            j = me + 4 * k
            arrive(j)

            @pl.when(row > 0)
            def _():
                hop_on(j, before, down_s)

            hop_on(j, across, side_s)
            fw_copy(j).start()

    landed(pair_video, pair_r.at[0])
    landed(pair_text, pair_r.at[1])

    def wait_q(k, c):
        j = lax.rem(across + n - 4 * k, n) // 2
        landed(q_all.at[j], q_r.at[j])
        return c

    lax.fori_loop(0, row_count, wait_q, 0)

    length = len_ref[0]
    key = lax.broadcasted_iota(jnp.int32, (1, 2 * positions + 2 * shard), 1)
    offset = key - 2 * positions
    token = jnp.where(offset < shard, me * shard + offset, partner * shard + offset - shard)
    key_ok = (offset < 0) | (token < length)
    lane = lax.broadcasted_iota(jnp.int32, (rows, 128), 1)
    stats = jnp.where(lane < 64, 0.0, 1.0).astype(f32)
    for h in range(heads):
        hs = slice(h * hd, (h + 1) * hd)
        q = q_all[:, :, hs].reshape(rows, hd)
        keys = jnp.concatenate(
            [video_ref[1, :, hs], pair_video[0, :, hs], text_ref[1, :, hs], pair_text[0, :, hs]],
            axis=0,
        )
        values = jnp.concatenate(
            [video_ref[2, :, hs], pair_video[1, :, hs], text_ref[2, :, hs], pair_text[1, :, hs]],
            axis=0,
        )
        s = jnp.where(key_ok, dot_nt(q, keys) * scale, masked_score)
        top, total, w = softmax_parts(s)
        part = dot_nn(w, values).astype(bf16).reshape(row_count, 2, shard, hd)
        for y in range(2):
            p_send[y, :, :, hs] = part[:, y]
        stats = jnp.where(lane == h, top, jnp.where(lane == h + 64, total, stats))
    stats = stats.reshape(row_count, 2, shard, 128)
    for y in range(2):
        m_send[y] = stats[:, y]

    column = lax.rem(mine, 2)
    across_copies = (
        remote(p_send.at[1 - column], p_mid, pa_s.at[0], pa_r.at[0], across),
        remote(m_send.at[1 - column], m_mid, pa_s.at[1], pa_r.at[1], across),
    )
    for copy in across_copies:
        copy.start()
    landed(p_mid, pa_r.at[0])
    landed(m_mid, pa_r.at[1])
    for z in range(row_count):
        ours, theirs = m_send[column, z], m_mid[z]
        best = jnp.maximum(ours, theirs)
        w_ours, w_theirs = jnp.exp(ours - best), jnp.exp(theirs - best)
        total = pltpu.roll(w_ours, 64, 1) * ours + pltpu.roll(w_theirs, 64, 1) * theirs
        m_out[z] = jnp.where(lax.broadcasted_iota(jnp.int32, best.shape, 1) < 64, best, total)
        for h in range(heads):
            hs = slice(h * hd, (h + 1) * hd)
            p_out[z, :, hs] = (
                w_ours[:, h : h + 1] * p_send[column, z, :, hs].astype(f32)
                + w_theirs[:, h : h + 1] * p_mid[z, :, hs].astype(f32)
            ).astype(bf16)

    def p_copy(to):
        z = to // 4
        return remote(p_out.at[z], p_recv.at[row], p_s.at[z], p_r.at[row], to)

    def m_copy(to):
        z = to // 4
        return remote(m_out.at[z], m_recv.at[row], m_s.at[z], m_r.at[row], to)

    def start_p(k, c):
        p_copy(along(k)).start()
        m_copy(along(k)).start()
        return c

    lax.fori_loop(1, row_count, start_p, 0)
    p_recv[row] = p_out[row]
    m_recv[row] = m_out[row]

    def wait_t(k, c):
        j = lax.rem(me + k, n)
        landed(t_recv.at[j], t_r.at[j])
        return c

    lax.fori_loop(1, n, wait_t, 0)
    count = n * piece
    row_at = lax.rem(lax.broadcasted_iota(jnp.int32, (count, count), 0), piece)
    col_at = lax.rem(lax.broadcasted_iota(jnp.int32, (count, count), 1), piece)
    same = row_at == col_at
    for i in range(half):
        hs = slice(i * hd, (i + 1) * hd)
        q, k_, v = (
            t_recv[:, t, :, hs].astype(f32).reshape(count, hd).astype(bf16) for t in range(3)
        )
        s = jnp.where(same, dot_nt(q, k_) * scale, masked_score)
        top, total, w = softmax_parts(s)
        o = dot_nn(w, v) / total
        o_send[:, :, hs] = o.reshape(n, piece, hd).astype(bf16)

    def o_copy(to):
        return remote(o_send.at[to], o_recv.at[me], o_s.at[to], o_r.at[me], to)

    def start_o(k, c):
        o_copy(lax.rem(me + k, n)).start()
        return c

    lax.fori_loop(1, n, start_o, 0)
    o_recv[me] = o_send[me]

    def forward(k, c):
        j = lax.rem(across + n - 4 * k, n)
        landed(kv_all.at[j], kv_r.at[j])
        fw_copy(j).start()
        return c

    lax.fori_loop(0, row_count, forward, 0)

    def wait_kv(k, c):
        j = lax.rem(partner + 2 * k, n)
        landed(kv_all.at[j], kv_r.at[j])
        return c

    lax.fori_loop(0, twins, wait_kv, 0)
    text_key = lax.broadcasted_iota(jnp.int32, (1, positions + text_total), 1) - positions
    joint_ok = text_key < length
    for i in range(half):
        q, k_, v = (in_slot(i, lambda c: video_ref[t, :, c]) for t in range(3))
        hs = slice(i * hd, (i + 1) * hd)
        keys = jnp.concatenate(
            [k_, kv_all[:, 0, :, hs].reshape(text_total, hd)], axis=0
        )
        values = jnp.concatenate(
            [v, kv_all[:, 1, :, hs].reshape(text_total, hd)], axis=0
        )
        s = jnp.where(joint_ok, dot_nt(q, keys) * scale, masked_score)
        top, total, w = softmax_parts(s)
        result[i] = (dot_nn(w, values) / total).astype(bf16)

    for h in range(heads):
        block = result[max(0, h - half)]
        for i in range(max(0, h - half) + 1, min(h, half - 1) + 1):
            block = jnp.where(places[h] == i, result[i], block)
        video_out[:, h * hd : (h + 1) * hd] = block

    def wait_p(k, c):
        j = along(k) // 4
        landed(p_recv.at[j], p_r.at[j])
        landed(m_recv.at[j], m_r.at[j])
        return c

    lax.fori_loop(1, row_count, wait_p, 0)
    tops = m_recv[...]
    sums = pltpu.roll(tops.reshape(row_count * shard, 128), 64, 1).reshape(tops.shape)
    best = tops.max(0, keepdims=True)
    weight = jnp.exp(jnp.minimum(tops - best, 0.0))
    total = (weight * sums).sum(0)
    for h in range(heads):
        hs = slice(h * hd, (h + 1) * hd)
        merged = (weight[:, :, h : h + 1] * p_recv[:, :, hs].astype(f32)).sum(0)
        text_out[:, hs] = (merged / total[:, h : h + 1]).astype(bf16)

    def wait_o(k, c):
        j = lax.rem(me + k, n)
        landed(o_recv.at[j], o_r.at[j])
        return c

    lax.fori_loop(1, n, wait_o, 0)
    for i in range(half):
        hs = slice(i * hd, (i + 1) * hd)
        result[half + i] = o_recv[:, :, hs].astype(f32).reshape(positions, hd).astype(bf16)
    for h in range(heads):
        hs = slice(h * hd, (h + 1) * hd)
        block = video_out[:, hs]
        for i in range(max(0, h - half), min(h, half - 1) + 1):
            block = jnp.where(places[h] == half + i, result[half + i], block)
        video_out[:, hs] = block

    sent(pair_video, pair_s.at[0])
    sent(pair_text, pair_s.at[1])
    sent(kv_all.at[me], fw_s.at[mine])

    for copy in across_copies:
        copy.wait_send()

    def gone(sems, j):
        sent(q_all.at[mine], sems.at[0, j])
        sent(kv_all.at[me], sems.at[1, j])

    for z in range(row_count):
        gone(side_s, z)

        @pl.when((z <= row) & (row < row_count - 1))
        def _():
            gone(up_s, z)

        @pl.when((z >= row) & (row > 0))
        def _():
            gone(down_s, z)

    def drain_row(k, c):
        j = along(k)
        sent(kv_all.at[me], fw_s.at[j // 2])
        sent(p_out.at[0], p_s.at[j // 4])
        sent(m_out.at[0], m_s.at[j // 4])
        return c

    lax.fori_loop(1, row_count, drain_row, 0)

    def drain_across(k, c):
        j = lax.rem(across + 4 * k, n)
        sent(kv_all.at[me], fw_s.at[j // 2])
        return c

    lax.fori_loop(0, row_count, drain_across, 0)

    def drain_all(k, c):
        j = lax.rem(me + k, n)
        sent(t_send.at[j], t_s.at[j])
        sent(o_send.at[j], o_s.at[j])
        return c

    lax.fori_loop(1, n, drain_all, 0)


def fused_body(n, video_qkv, text_qkv, head_kind, text_len):
    heads = head_kind.shape[0]
    _, _, positions, width = video_qkv.shape
    shard = text_qkv.shape[1]
    half, twins, piece = heads // 2, n // 2, positions // n
    hd = width // heads
    narrow = half * hd
    rows = n // 4
    vmem = pl.BlockSpec(memory_space=pltpu.VMEM)
    hbm = pl.BlockSpec(memory_space=pltpu.HBM)
    dma = pltpu.SemaphoreType.DMA
    video_out, text_out = pl.pallas_call(
        functools.partial(kernel, n, heads),
        out_shape=(
            jax.ShapeDtypeStruct((positions, width), bf16),
            jax.ShapeDtypeStruct((shard, width), bf16),
        ),
        in_specs=[hbm] * 4,
        out_specs=(vmem, vmem),
        scratch_shapes=[
            pltpu.SMEM((heads,), jnp.int32),
            pltpu.SMEM((1,), jnp.int32),
            pltpu.VMEM((3, positions, width), bf16),
            pltpu.VMEM((3, shard, width), bf16),
            pltpu.VMEM((2, positions, width), bf16),
            pltpu.VMEM((2, shard, width), bf16),
            pltpu.VMEM((twins, shard, width), bf16),
            pltpu.VMEM((n, 2, shard, narrow), bf16),
            pltpu.VMEM((n, 3, piece, narrow), bf16),
            pltpu.VMEM((n, 3, piece, narrow), bf16),
            pltpu.VMEM((n, piece, narrow), bf16),
            pltpu.VMEM((n, piece, narrow), bf16),
            pltpu.VMEM((2, rows, shard, width), bf16),
            pltpu.VMEM((rows, shard, width), bf16),
            pltpu.VMEM((rows, shard, width), bf16),
            pltpu.VMEM((rows, shard, width), bf16),
            pltpu.VMEM((2, rows, shard, 128), f32),
            pltpu.VMEM((rows, shard, 128), f32),
            pltpu.VMEM((rows, shard, 128), f32),
            pltpu.VMEM((rows, shard, 128), f32),
            pltpu.VMEM((heads, positions, hd), bf16),
            dma((4,)),
            dma((2,)),
            dma((2,)),
            dma((2, rows)),
            dma((2, rows)),
            dma((2, rows)),
            dma((twins,)),
            dma((n,)),
            dma((twins,)),
            dma((n,)),
            dma((n,)),
            dma((n,)),
            dma((n,)),
            dma((2,)),
            dma((2,)),
            dma((rows,)),
            dma((rows,)),
            dma((rows,)),
            dma((rows,)),
        ],
        compiler_params=pltpu.CompilerParams(
            collective_id=0, has_side_effects=True, vmem_limit_bytes=63 << 20
        ),
    )(head_kind, text_len, video_qkv.reshape(3, positions, width), text_qkv)
    return video_out.reshape(1, positions, width), text_out


def body(n, video_qkv, text_qkv, head_kind, text_len):
    heads = head_kind.shape[0]
    positions, width = video_qkv.shape[2:]
    shard = text_qkv.shape[1]
    whole_tiles = (
        video_qkv.shape[1] == 1
        and n % 4 == 0
        and heads % 2 == 0
        and heads <= 64
        and shard % 16 == 0
        and positions % (8 * n) == 0
        and (width // heads) % 128 == 0
    )
    if whole_tiles:
        return fused_body(n, video_qkv, text_qkv, head_kind, text_len)
    return plain_body(video_qkv, text_qkv, head_kind, text_len)


def solution(mesh):
    in_specs = (
        P(None, ("groups", "frame"), None, None),
        P(None, ("groups", "frame"), None),
        P("groups"),
        P("groups"),
    )
    out_specs = (P(("groups", "frame"), None, None), P(("groups", "frame"), None))
    return jax.shard_map(
        functools.partial(body, mesh.shape["frame"]), mesh=mesh, in_specs=in_specs, out_specs=out_specs, check_vma=False)
```

```python
import functools

import jax
import jax.numpy as jnp
from jax import lax
from jax.experimental import pallas as pl
from jax.experimental.pallas import tpu as pltpu
from jax.sharding import PartitionSpec as P

masked_score = -1e30


def plain_body(video_qkv, text_qkv, head_kind, text_len):
    head_count = head_kind.shape[0]
    head_width = video_qkv.shape[-1]
    head_dim = head_width // head_count
    positions = video_qkv.shape[2]
    shard_text = text_qkv.shape[1]
    score_scale = head_dim ** (-0.5)
    device_rank = lax.axis_index("frame")
    local_video = video_qkv.reshape(3, 1, positions, head_count, head_dim)
    gathered = lax.all_gather(text_qkv, "frame", axis=1, tiled=True)
    text_total = gathered.shape[1]
    all_text = gathered.reshape(3, text_total, head_count, head_dim)
    text_valid = jnp.arange(text_total) < text_len[0]
    spatial_heads = jnp.nonzero(head_kind == 0, size=head_count - head_count // 2)[0].astype(
        jnp.int32
    )
    temporal_heads = jnp.nonzero(head_kind == 1, size=head_count // 2)[0].astype(jnp.int32)
    own_frame = jnp.take(local_video[:, 0], spatial_heads, axis=2)
    text_spatial = jnp.take(all_text[1:], spatial_heads, axis=2)
    joint_keys = jnp.concatenate([own_frame[1], text_spatial[0]], axis=0)
    joint_values = jnp.concatenate([own_frame[2], text_spatial[1]], axis=0)
    joint_valid = jnp.concatenate([jnp.ones((positions,), bool), text_valid])
    spatial_scores = (
        jnp.einsum("phd,khd->hpk", own_frame[0], joint_keys, preferred_element_type=jnp.float32)
        * score_scale
    )
    spatial_scores = jnp.where(joint_valid, spatial_scores, masked_score)
    row_max = spatial_scores.max(-1, keepdims=True)
    spatial_exp = jnp.exp(spatial_scores - row_max)
    totals = spatial_exp.sum(-1)
    summed = jnp.einsum(
        "hpk,khd->phd",
        spatial_exp.astype(jnp.bfloat16),
        joint_values,
        preferred_element_type=jnp.float32,
    )
    spatial_result = (summed / totals.T[..., None]).astype(jnp.bfloat16)
    selected = jnp.take(local_video, temporal_heads, axis=3)
    block = lax.all_to_all(selected, "frame", split_axis=2, concat_axis=1, tiled=True)
    scores = (
        jnp.einsum("fphd,gphd->phfg", block[0], block[1], preferred_element_type=jnp.float32)
        * score_scale
    )
    block_max = scores.max(-1, keepdims=True)
    exps = jnp.exp(scores - block_max)
    block_totals = exps.sum(-1)
    block_sum = jnp.einsum(
        "phfg,gphd->fphd", exps.astype(jnp.bfloat16), block[2], preferred_element_type=jnp.float32
    )
    result = (block_sum / jnp.transpose(block_totals, (2, 0, 1))[..., None]).astype(jnp.bfloat16)
    temporal_result = lax.all_to_all(result, "frame", split_axis=0, concat_axis=1, tiled=True)[0]
    joined = jnp.concatenate([spatial_result, temporal_result], axis=1)
    order = jnp.concatenate([spatial_heads, temporal_heads])
    inverse = jnp.argsort(order)
    video_out = jnp.take(joined, inverse, axis=1).reshape(1, positions, head_width)
    text_queries = all_text[0]
    own_text = text_qkv.reshape(3, shard_text, head_count, head_dim)
    own_valid = device_rank * shard_text + jnp.arange(shard_text) < text_len[0]
    local_keys = jnp.concatenate([local_video[1, 0], own_text[1]], axis=0)
    local_values = jnp.concatenate([local_video[2, 0], own_text[2]], axis=0)
    local_valid = jnp.concatenate([jnp.ones((positions,), bool), own_valid])
    query_scores = (
        jnp.einsum("thd,khd->thk", text_queries, local_keys, preferred_element_type=jnp.float32)
        * score_scale
    )
    query_scores = jnp.where(local_valid, query_scores, masked_score)
    local_max = query_scores.max(-1)
    global_max = lax.pmax(local_max, "frame")
    query_exp = jnp.exp(query_scores - global_max[..., None])
    query_totals = query_exp.sum(-1)
    query_sums = jnp.einsum(
        "thk,khd->thd",
        query_exp.astype(jnp.bfloat16),
        local_values,
        preferred_element_type=jnp.float32,
    )
    query_totals, query_sums = (query_totals, query_sums)
    query_sums, query_totals = (
        lax.psum_scatter(query_sums, "frame", scatter_dimension=0, tiled=True),
        lax.psum_scatter(query_totals, "frame", scatter_dimension=0, tiled=True),
    )
    text_out = (
        (query_sums / query_totals[..., None]).astype(jnp.bfloat16).reshape(shard_text, head_width)
    )
    return (video_out, text_out)


f32 = jnp.float32
bf16 = jnp.bfloat16


def dot_nt(a, b):
    return lax.dot_general(a, b, (((1,), (1,)), ((), ())), preferred_element_type=f32)


def dot_nn(a, b):
    return lax.dot_general(a, b, (((1,), (0,)), ((), ())), preferred_element_type=f32)


def softmax_parts(scores):
    top = scores.max(-1, keepdims=True)
    e = jnp.exp(scores - top)
    return top, e.sum(-1, keepdims=True), e.astype(bf16)


def remote(src, dst, send_sem, recv_sem, peer):
    return pltpu.make_async_remote_copy(
        src_ref=src,
        dst_ref=dst,
        send_sem=send_sem,
        recv_sem=recv_sem,
        device_id={"frame": peer},
        device_id_type=pl.DeviceIdType.MESH,
    )


def kernel(
    n,
    heads,
    kind_hbm,
    len_hbm,
    video_hbm,
    text_hbm,
    video_out,
    text_out,
    kind_ref,
    len_ref,
    video_ref,
    text_ref,
    pair_video,
    pair_text,
    q_all,
    kv_all,
    t_send,
    t_recv,
    o_send,
    o_recv,
    p_send,
    p_mid,
    p_out,
    p_recv,
    m_send,
    m_mid,
    m_out,
    m_recv,
    result,
    in_sem,
    pair_s,
    pair_r,
    up_s,
    down_s,
    side_s,
    q_r,
    kv_r,
    fw_s,
    t_s,
    t_r,
    o_s,
    o_r,
    pa_s,
    pa_r,
    p_s,
    p_r,
    m_s,
    m_r,
):
    half = heads // 2
    twins = n // 2
    positions = video_ref.shape[1]
    hd = video_ref.shape[2] // heads
    shard = text_ref.shape[1]
    piece = positions // n
    text_total = n * shard
    rows = twins * shard
    scale = hd ** (-0.5)
    me = lax.axis_index("frame")
    parity = lax.rem(me, 2)
    across = me + 2 - 4 * lax.rem(me // 2, 2)
    row_count = n // 4
    partner = me + 1 - 2 * parity
    mine = me // 2

    barrier = pltpu.get_barrier_semaphore()

    def greet(k, c):
        pl.semaphore_signal(
            barrier,
            inc=1,
            device_id={"frame": lax.rem(me + k, n)},
            device_id_type=pl.DeviceIdType.MESH,
        )
        return c

    inputs = [
        pltpu.make_async_copy(a, b, in_sem.at[i])
        for i, (a, b) in enumerate(
            (
                (kind_hbm, kind_ref),
                (len_hbm, len_ref),
                (text_hbm, text_ref),
                (video_hbm, video_ref),
            )
        )
    ]
    for copy in inputs:
        copy.start()
    lax.fori_loop(1, n, greet, 0)
    for copy in inputs:
        copy.wait()

    spatial_seen = jnp.int32(0)
    temporal_seen = jnp.int32(0)
    places = []
    for h in range(heads):
        kind = kind_ref[h]
        place = jnp.where(kind == 0, spatial_seen, half + temporal_seen)
        places.append(place)
        spatial_seen = spatial_seen + jnp.where(kind == 0, 1, 0)
        temporal_seen = temporal_seen + jnp.where(kind == 0, 0, 1)

    def in_slot(i, load):
        first = i % half
        block = load(slice(first * hd, (first + 1) * hd))
        for h in range(first + 1, first + half + 1):
            block = jnp.where(places[h] == i, load(slice(h * hd, (h + 1) * hd)), block)
        return block

    for i in range(half):
        for t in range(2):
            kv_all[me, t, :, i * hd : (i + 1) * hd] = in_slot(i, lambda c: text_ref[t + 1, :, c])
    q_all[mine] = text_ref[0]

    for i in range(half):
        for t in range(3):
            whole = in_slot(half + i, lambda c: video_ref[t, :, c])
            whole = whole.astype(f32).reshape(n, piece, hd)
            t_send[:, t, :, i * hd : (i + 1) * hd] = whole.astype(bf16)

    pl.semaphore_wait(barrier, n - 1)

    def pair_copies():
        return (
            remote(video_hbm.at[1:3], pair_video, pair_s.at[0], pair_r.at[0], partner),
            remote(text_hbm.at[1:3], pair_text, pair_s.at[1], pair_r.at[1], partner),
            remote(kv_all.at[me], kv_all.at[me], fw_s.at[mine], kv_r.at[me], partner),
        )

    for c in pair_copies():
        c.start()

    def along(k):
        return lax.rem(me + 4 * k, n)

    def t_copy(to):
        return remote(t_send.at[to], t_recv.at[me], t_s.at[to], t_r.at[me], to)

    def landed(dst, sem):
        remote(dst, dst, sem, sem, partner).wait_recv()

    def sent(src, sem):
        remote(src, src, sem, sem, partner).wait_send()

    def start_t(k, c):
        t_copy(lax.rem(me + k, n)).start()
        return c

    row = me // 4
    after, before = me + 4, me - 4

    def hop(j, to, sems):
        d = j // 2
        return (
            remote(q_all.at[d], q_all.at[d], sems.at[0, j // 4], q_r.at[d], to),
            remote(kv_all.at[j], kv_all.at[j], sems.at[1, j // 4], kv_r.at[j], to),
        )

    def fw_copy(j):
        return remote(kv_all.at[j], kv_all.at[j], fw_s.at[j // 2], kv_r.at[j], partner)

    def hop_on(j, to, sems):
        for copy in hop(j, to, sems):
            copy.start()

    @pl.when(row < row_count - 1)
    def _():
        hop_on(me, after, up_s)

    @pl.when(row > 0)
    def _():
        hop_on(me, before, down_s)

    hop_on(me, across, side_s)

    def arrive(j):
        landed(q_all.at[j // 2], q_r.at[j // 2])
        landed(kv_all.at[j], kv_r.at[j])

    for k in range(1, row_count):

        @pl.when(row >= k)
        def _():
            j = me - 4 * k
            arrive(j)

            @pl.when(row < row_count - 1)
            def _():
                hop_on(j, after, up_s)

            hop_on(j, across, side_s)
            fw_copy(j).start()

        @pl.when(row + k < row_count)
        def _():
            j = me + 4 * k
            arrive(j)

            @pl.when(row > 0)
            def _():
                hop_on(j, before, down_s)

            hop_on(j, across, side_s)
            fw_copy(j).start()

    lax.fori_loop(1, n, start_t, 0)
    t_recv[me] = t_send[me]
    landed(pair_video, pair_r.at[0])
    landed(pair_text, pair_r.at[1])

    def wait_q(k, c):
        j = lax.rem(across + n - 4 * k, n) // 2
        landed(q_all.at[j], q_r.at[j])
        return c

    lax.fori_loop(0, row_count, wait_q, 0)

    length = len_ref[0]
    key = lax.broadcasted_iota(jnp.int32, (1, 2 * positions + 2 * shard), 1)
    offset = key - 2 * positions
    token = jnp.where(offset < shard, me * shard + offset, partner * shard + offset - shard)
    key_ok = (offset < 0) | (token < length)
    lane = lax.broadcasted_iota(jnp.int32, (rows, 128), 1)
    stats = jnp.where(lane < 64, 0.0, 1.0).astype(f32)
    for h in range(heads):
        hs = slice(h * hd, (h + 1) * hd)
        q = q_all[:, :, hs].reshape(rows, hd)
        keys = jnp.concatenate(
            [video_ref[1, :, hs], pair_video[0, :, hs], text_ref[1, :, hs], pair_text[0, :, hs]],
            axis=0,
        )
        values = jnp.concatenate(
            [video_ref[2, :, hs], pair_video[1, :, hs], text_ref[2, :, hs], pair_text[1, :, hs]],
            axis=0,
        )
        s = jnp.where(key_ok, dot_nt(q, keys) * scale, masked_score)
        top, total, w = softmax_parts(s)
        part = dot_nn(w, values).astype(bf16).reshape(row_count, 2, shard, hd)
        for y in range(2):
            p_send[y, :, :, hs] = part[:, y]
        stats = jnp.where(lane == h, top, jnp.where(lane == h + 64, total, stats))
    stats = stats.reshape(row_count, 2, shard, 128)
    for y in range(2):
        m_send[y] = stats[:, y]

    column = lax.rem(mine, 2)
    across_copies = (
        remote(p_send.at[1 - column], p_mid, pa_s.at[0], pa_r.at[0], across),
        remote(m_send.at[1 - column], m_mid, pa_s.at[1], pa_r.at[1], across),
    )
    for copy in across_copies:
        copy.start()
    def wait_t(k, c):
        j = lax.rem(me + k, n)
        landed(t_recv.at[j], t_r.at[j])
        return c

    lax.fori_loop(1, n, wait_t, 0)
    count = n * piece
    row_at = lax.rem(lax.broadcasted_iota(jnp.int32, (count, count), 0), piece)
    col_at = lax.rem(lax.broadcasted_iota(jnp.int32, (count, count), 1), piece)
    same = row_at == col_at
    for i in range(half):
        hs = slice(i * hd, (i + 1) * hd)
        q, k_, v = (
            t_recv[:, t, :, hs].astype(f32).reshape(count, hd).astype(bf16) for t in range(3)
        )
        s = jnp.where(same, dot_nt(q, k_) * scale, masked_score)
        top, total, w = softmax_parts(s)
        o = dot_nn(w, v) / total
        o_send[:, :, hs] = o.reshape(n, piece, hd).astype(bf16)

    def o_copy(to):
        return remote(o_send.at[to], o_recv.at[me], o_s.at[to], o_r.at[me], to)

    def start_o(k, c):
        o_copy(lax.rem(me + k, n)).start()
        return c

    lax.fori_loop(1, n, start_o, 0)
    o_recv[me] = o_send[me]

    landed(p_mid, pa_r.at[0])
    landed(m_mid, pa_r.at[1])
    for z in range(row_count):
        ours, theirs = m_send[column, z], m_mid[z]
        best = jnp.maximum(ours, theirs)
        w_ours, w_theirs = jnp.exp(ours - best), jnp.exp(theirs - best)
        total = pltpu.roll(w_ours, 64, 1) * ours + pltpu.roll(w_theirs, 64, 1) * theirs
        m_out[z] = jnp.where(lax.broadcasted_iota(jnp.int32, best.shape, 1) < 64, best, total)
        for h in range(heads):
            hs = slice(h * hd, (h + 1) * hd)
            p_out[z, :, hs] = (
                w_ours[:, h : h + 1] * p_send[column, z, :, hs].astype(f32)
                + w_theirs[:, h : h + 1] * p_mid[z, :, hs].astype(f32)
            ).astype(bf16)

    def p_copy(to):
        z = to // 4
        return remote(p_out.at[z], p_recv.at[row], p_s.at[z], p_r.at[row], to)

    def m_copy(to):
        z = to // 4
        return remote(m_out.at[z], m_recv.at[row], m_s.at[z], m_r.at[row], to)

    def start_p(k, c):
        p_copy(along(k)).start()
        m_copy(along(k)).start()
        return c

    lax.fori_loop(1, row_count, start_p, 0)
    p_recv[row] = p_out[row]
    m_recv[row] = m_out[row]

    def forward(k, c):
        j = lax.rem(across + n - 4 * k, n)
        landed(kv_all.at[j], kv_r.at[j])
        fw_copy(j).start()
        return c

    lax.fori_loop(0, row_count, forward, 0)

    def wait_kv(k, c):
        j = lax.rem(partner + 2 * k, n)
        landed(kv_all.at[j], kv_r.at[j])
        return c

    lax.fori_loop(0, twins, wait_kv, 0)
    text_key = lax.broadcasted_iota(jnp.int32, (1, positions + text_total), 1) - positions
    joint_ok = text_key < length
    for i in range(half):
        q, k_, v = (in_slot(i, lambda c: video_ref[t, :, c]) for t in range(3))
        hs = slice(i * hd, (i + 1) * hd)
        keys = jnp.concatenate(
            [k_, kv_all[:, 0, :, hs].reshape(text_total, hd)], axis=0
        )
        values = jnp.concatenate(
            [v, kv_all[:, 1, :, hs].reshape(text_total, hd)], axis=0
        )
        s = jnp.where(joint_ok, dot_nt(q, keys) * scale, masked_score)
        top, total, w = softmax_parts(s)
        result[i] = (dot_nn(w, values) / total).astype(bf16)

    for h in range(heads):
        block = result[max(0, h - half)]
        for i in range(max(0, h - half) + 1, min(h, half - 1) + 1):
            block = jnp.where(places[h] == i, result[i], block)
        video_out[:, h * hd : (h + 1) * hd] = block

    def wait_p(k, c):
        j = along(k) // 4
        landed(p_recv.at[j], p_r.at[j])
        landed(m_recv.at[j], m_r.at[j])
        return c

    lax.fori_loop(1, row_count, wait_p, 0)
    tops = m_recv[...]
    sums = pltpu.roll(tops.reshape(row_count * shard, 128), 64, 1).reshape(tops.shape)
    best = tops.max(0, keepdims=True)
    weight = jnp.exp(jnp.minimum(tops - best, 0.0))
    total = (weight * sums).sum(0)
    for h in range(heads):
        hs = slice(h * hd, (h + 1) * hd)
        merged = (weight[:, :, h : h + 1] * p_recv[:, :, hs].astype(f32)).sum(0)
        text_out[:, hs] = (merged / total[:, h : h + 1]).astype(bf16)

    def wait_o(k, c):
        j = lax.rem(me + k, n)
        landed(o_recv.at[j], o_r.at[j])
        return c

    lax.fori_loop(1, n, wait_o, 0)
    for i in range(half):
        hs = slice(i * hd, (i + 1) * hd)
        result[half + i] = o_recv[:, :, hs].astype(f32).reshape(positions, hd).astype(bf16)
    for h in range(heads):
        hs = slice(h * hd, (h + 1) * hd)
        block = video_out[:, hs]
        for i in range(max(0, h - half), min(h, half - 1) + 1):
            block = jnp.where(places[h] == half + i, result[half + i], block)
        video_out[:, hs] = block

    sent(pair_video, pair_s.at[0])
    sent(pair_text, pair_s.at[1])
    sent(kv_all.at[me], fw_s.at[mine])

    for copy in across_copies:
        copy.wait_send()

    def gone(sems, j):
        sent(q_all.at[mine], sems.at[0, j])
        sent(kv_all.at[me], sems.at[1, j])

    for z in range(row_count):
        gone(side_s, z)

        @pl.when((z <= row) & (row < row_count - 1))
        def _():
            gone(up_s, z)

        @pl.when((z >= row) & (row > 0))
        def _():
            gone(down_s, z)

    def drain_row(k, c):
        j = along(k)
        sent(kv_all.at[me], fw_s.at[j // 2])
        sent(p_out.at[0], p_s.at[j // 4])
        sent(m_out.at[0], m_s.at[j // 4])
        return c

    lax.fori_loop(1, row_count, drain_row, 0)

    def drain_across(k, c):
        j = lax.rem(across + 4 * k, n)
        sent(kv_all.at[me], fw_s.at[j // 2])
        return c

    lax.fori_loop(0, row_count, drain_across, 0)

    def drain_all(k, c):
        j = lax.rem(me + k, n)
        sent(t_send.at[j], t_s.at[j])
        sent(o_send.at[j], o_s.at[j])
        return c

    lax.fori_loop(1, n, drain_all, 0)


def fused_body(n, video_qkv, text_qkv, head_kind, text_len):
    heads = head_kind.shape[0]
    _, _, positions, width = video_qkv.shape
    shard = text_qkv.shape[1]
    half, twins, piece = heads // 2, n // 2, positions // n
    hd = width // heads
    narrow = half * hd
    rows = n // 4
    vmem = pl.BlockSpec(memory_space=pltpu.VMEM)
    hbm = pl.BlockSpec(memory_space=pltpu.HBM)
    dma = pltpu.SemaphoreType.DMA
    video_out, text_out = pl.pallas_call(
        functools.partial(kernel, n, heads),
        out_shape=(
            jax.ShapeDtypeStruct((positions, width), bf16),
            jax.ShapeDtypeStruct((shard, width), bf16),
        ),
        in_specs=[hbm] * 4,
        out_specs=(vmem, vmem),
        scratch_shapes=[
            pltpu.SMEM((heads,), jnp.int32),
            pltpu.SMEM((1,), jnp.int32),
            pltpu.VMEM((3, positions, width), bf16),
            pltpu.VMEM((3, shard, width), bf16),
            pltpu.VMEM((2, positions, width), bf16),
            pltpu.VMEM((2, shard, width), bf16),
            pltpu.VMEM((twins, shard, width), bf16),
            pltpu.VMEM((n, 2, shard, narrow), bf16),
            pltpu.VMEM((n, 3, piece, narrow), bf16),
            pltpu.VMEM((n, 3, piece, narrow), bf16),
            pltpu.VMEM((n, piece, narrow), bf16),
            pltpu.VMEM((n, piece, narrow), bf16),
            pltpu.VMEM((2, rows, shard, width), bf16),
            pltpu.VMEM((rows, shard, width), bf16),
            pltpu.VMEM((rows, shard, width), bf16),
            pltpu.VMEM((rows, shard, width), bf16),
            pltpu.VMEM((2, rows, shard, 128), f32),
            pltpu.VMEM((rows, shard, 128), f32),
            pltpu.VMEM((rows, shard, 128), f32),
            pltpu.VMEM((rows, shard, 128), f32),
            pltpu.VMEM((heads, positions, hd), bf16),
            dma((4,)),
            dma((2,)),
            dma((2,)),
            dma((2, rows)),
            dma((2, rows)),
            dma((2, rows)),
            dma((twins,)),
            dma((n,)),
            dma((twins,)),
            dma((n,)),
            dma((n,)),
            dma((n,)),
            dma((n,)),
            dma((2,)),
            dma((2,)),
            dma((rows,)),
            dma((rows,)),
            dma((rows,)),
            dma((rows,)),
        ],
        compiler_params=pltpu.CompilerParams(
            collective_id=0, has_side_effects=True, vmem_limit_bytes=63 << 20
        ),
    )(head_kind, text_len, video_qkv.reshape(3, positions, width), text_qkv)
    return video_out.reshape(1, positions, width), text_out


def body(n, video_qkv, text_qkv, head_kind, text_len):
    heads = head_kind.shape[0]
    positions, width = video_qkv.shape[2:]
    shard = text_qkv.shape[1]
    whole_tiles = (
        video_qkv.shape[1] == 1
        and n % 4 == 0
        and heads % 2 == 0
        and heads <= 64
        and shard % 16 == 0
        and positions % (8 * n) == 0
        and (width // heads) % 128 == 0
    )
    if whole_tiles:
        return fused_body(n, video_qkv, text_qkv, head_kind, text_len)
    return plain_body(video_qkv, text_qkv, head_kind, text_len)


def solution(mesh):
    in_specs = (
        P(None, ("groups", "frame"), None, None),
        P(None, ("groups", "frame"), None),
        P("groups"),
        P("groups"),
    )
    out_specs = (P(("groups", "frame"), None, None), P(("groups", "frame"), None))
    return jax.shard_map(
        functools.partial(body, mesh.shape["frame"]), mesh=mesh, in_specs=in_specs, out_specs=out_specs, check_vma=False)
```

```python
import functools

import jax
import jax.numpy as jnp
from jax import lax
from jax.experimental import pallas as pl
from jax.experimental.pallas import tpu as pltpu
from jax.sharding import PartitionSpec as P

masked_score = -1e30


def plain_body(video_qkv, text_qkv, head_kind, text_len):
    head_count = head_kind.shape[0]
    head_width = video_qkv.shape[-1]
    head_dim = head_width // head_count
    positions = video_qkv.shape[2]
    shard_text = text_qkv.shape[1]
    score_scale = head_dim ** (-0.5)
    device_rank = lax.axis_index("frame")
    local_video = video_qkv.reshape(3, 1, positions, head_count, head_dim)
    gathered = lax.all_gather(text_qkv, "frame", axis=1, tiled=True)
    text_total = gathered.shape[1]
    all_text = gathered.reshape(3, text_total, head_count, head_dim)
    text_valid = jnp.arange(text_total) < text_len[0]
    spatial_heads = jnp.nonzero(head_kind == 0, size=head_count - head_count // 2)[0].astype(
        jnp.int32
    )
    temporal_heads = jnp.nonzero(head_kind == 1, size=head_count // 2)[0].astype(jnp.int32)
    own_frame = jnp.take(local_video[:, 0], spatial_heads, axis=2)
    text_spatial = jnp.take(all_text[1:], spatial_heads, axis=2)
    joint_keys = jnp.concatenate([own_frame[1], text_spatial[0]], axis=0)
    joint_values = jnp.concatenate([own_frame[2], text_spatial[1]], axis=0)
    joint_valid = jnp.concatenate([jnp.ones((positions,), bool), text_valid])
    spatial_scores = (
        jnp.einsum("phd,khd->hpk", own_frame[0], joint_keys, preferred_element_type=jnp.float32)
        * score_scale
    )
    spatial_scores = jnp.where(joint_valid, spatial_scores, masked_score)
    row_max = spatial_scores.max(-1, keepdims=True)
    spatial_exp = jnp.exp(spatial_scores - row_max)
    totals = spatial_exp.sum(-1)
    summed = jnp.einsum(
        "hpk,khd->phd",
        spatial_exp.astype(jnp.bfloat16),
        joint_values,
        preferred_element_type=jnp.float32,
    )
    spatial_result = (summed / totals.T[..., None]).astype(jnp.bfloat16)
    selected = jnp.take(local_video, temporal_heads, axis=3)
    block = lax.all_to_all(selected, "frame", split_axis=2, concat_axis=1, tiled=True)
    scores = (
        jnp.einsum("fphd,gphd->phfg", block[0], block[1], preferred_element_type=jnp.float32)
        * score_scale
    )
    block_max = scores.max(-1, keepdims=True)
    exps = jnp.exp(scores - block_max)
    block_totals = exps.sum(-1)
    block_sum = jnp.einsum(
        "phfg,gphd->fphd", exps.astype(jnp.bfloat16), block[2], preferred_element_type=jnp.float32
    )
    result = (block_sum / jnp.transpose(block_totals, (2, 0, 1))[..., None]).astype(jnp.bfloat16)
    temporal_result = lax.all_to_all(result, "frame", split_axis=0, concat_axis=1, tiled=True)[0]
    joined = jnp.concatenate([spatial_result, temporal_result], axis=1)
    order = jnp.concatenate([spatial_heads, temporal_heads])
    inverse = jnp.argsort(order)
    video_out = jnp.take(joined, inverse, axis=1).reshape(1, positions, head_width)
    text_queries = all_text[0]
    own_text = text_qkv.reshape(3, shard_text, head_count, head_dim)
    own_valid = device_rank * shard_text + jnp.arange(shard_text) < text_len[0]
    local_keys = jnp.concatenate([local_video[1, 0], own_text[1]], axis=0)
    local_values = jnp.concatenate([local_video[2, 0], own_text[2]], axis=0)
    local_valid = jnp.concatenate([jnp.ones((positions,), bool), own_valid])
    query_scores = (
        jnp.einsum("thd,khd->thk", text_queries, local_keys, preferred_element_type=jnp.float32)
        * score_scale
    )
    query_scores = jnp.where(local_valid, query_scores, masked_score)
    local_max = query_scores.max(-1)
    global_max = lax.pmax(local_max, "frame")
    query_exp = jnp.exp(query_scores - global_max[..., None])
    query_totals = query_exp.sum(-1)
    query_sums = jnp.einsum(
        "thk,khd->thd",
        query_exp.astype(jnp.bfloat16),
        local_values,
        preferred_element_type=jnp.float32,
    )
    query_totals, query_sums = (query_totals, query_sums)
    query_sums, query_totals = (
        lax.psum_scatter(query_sums, "frame", scatter_dimension=0, tiled=True),
        lax.psum_scatter(query_totals, "frame", scatter_dimension=0, tiled=True),
    )
    text_out = (
        (query_sums / query_totals[..., None]).astype(jnp.bfloat16).reshape(shard_text, head_width)
    )
    return (video_out, text_out)


f32 = jnp.float32
bf16 = jnp.bfloat16


def dot_nt(a, b):
    return lax.dot_general(a, b, (((1,), (1,)), ((), ())), preferred_element_type=f32)


def dot_nn(a, b):
    return lax.dot_general(a, b, (((1,), (0,)), ((), ())), preferred_element_type=f32)


def softmax_parts(scores):
    top = scores.max(-1, keepdims=True)
    e = jnp.exp(scores - top)
    return top, e.sum(-1, keepdims=True), e.astype(bf16)


def remote(src, dst, send_sem, recv_sem, peer):
    return pltpu.make_async_remote_copy(
        src_ref=src,
        dst_ref=dst,
        send_sem=send_sem,
        recv_sem=recv_sem,
        device_id={"frame": peer},
        device_id_type=pl.DeviceIdType.MESH,
    )


def kernel(
    n,
    heads,
    kind_hbm,
    len_hbm,
    video_hbm,
    text_hbm,
    video_out,
    text_out,
    kind_ref,
    len_ref,
    video_ref,
    text_ref,
    pair_video,
    pair_text,
    q_all,
    kv_all,
    t_send,
    t_recv,
    o_send,
    o_recv,
    p_send,
    p_mid,
    p_out,
    p_recv,
    m_send,
    m_mid,
    m_out,
    m_recv,
    result,
    in_sem,
    pair_s,
    pair_r,
    up_s,
    down_s,
    side_s,
    q_r,
    kv_r,
    fw_s,
    t_s,
    t_r,
    o_s,
    o_r,
    pa_s,
    pa_r,
    p_s,
    p_r,
    m_s,
    m_r,
):
    half = heads // 2
    twins = n // 2
    positions = video_ref.shape[1]
    hd = video_ref.shape[2] // heads
    shard = text_ref.shape[1]
    piece = positions // n
    text_total = n * shard
    rows = twins * shard
    scale = hd ** (-0.5)
    me = lax.axis_index("frame")
    parity = lax.rem(me, 2)
    across = me + 2 - 4 * lax.rem(me // 2, 2)
    row_count = n // 4
    partner = me + 1 - 2 * parity
    mine = me // 2

    barrier = pltpu.get_barrier_semaphore()

    def greet(k, c):
        pl.semaphore_signal(
            barrier,
            inc=1,
            device_id={"frame": lax.rem(me + k, n)},
            device_id_type=pl.DeviceIdType.MESH,
        )
        return c

    inputs = [
        pltpu.make_async_copy(a, b, in_sem.at[i])
        for i, (a, b) in enumerate(
            (
                (kind_hbm, kind_ref),
                (len_hbm, len_ref),
                (text_hbm, text_ref),
                (video_hbm, video_ref),
            )
        )
    ]
    for copy in inputs:
        copy.start()
    lax.fori_loop(1, n, greet, 0)
    for copy in inputs[:3]:
        copy.wait()

    spatial_seen = jnp.int32(0)
    temporal_seen = jnp.int32(0)
    places = []
    for h in range(heads):
        kind = kind_ref[h]
        place = jnp.where(kind == 0, spatial_seen, half + temporal_seen)
        places.append(place)
        spatial_seen = spatial_seen + jnp.where(kind == 0, 1, 0)
        temporal_seen = temporal_seen + jnp.where(kind == 0, 0, 1)

    def in_slot(i, load):
        first = i % half
        block = load(slice(first * hd, (first + 1) * hd))
        for h in range(first + 1, first + half + 1):
            block = jnp.where(places[h] == i, load(slice(h * hd, (h + 1) * hd)), block)
        return block

    for i in range(half):
        for t in range(2):
            kv_all[me, t, :, i * hd : (i + 1) * hd] = in_slot(i, lambda c: text_ref[t + 1, :, c])
    q_all[mine] = text_ref[0]

    pl.semaphore_wait(barrier, n - 1)

    def pair_copies():
        return (
            remote(video_hbm.at[1:3], pair_video, pair_s.at[0], pair_r.at[0], partner),
            remote(text_hbm.at[1:3], pair_text, pair_s.at[1], pair_r.at[1], partner),
            remote(kv_all.at[me], kv_all.at[me], fw_s.at[mine], kv_r.at[me], partner),
        )

    for c in pair_copies():
        c.start()

    def along(k):
        return lax.rem(me + 4 * k, n)

    def t_copy(to):
        return remote(t_send.at[to], t_recv.at[me], t_s.at[to], t_r.at[me], to)

    def landed(dst, sem):
        remote(dst, dst, sem, sem, partner).wait_recv()

    def sent(src, sem):
        remote(src, src, sem, sem, partner).wait_send()

    def start_t(k, c):
        t_copy(lax.rem(me + k, n)).start()
        return c

    row = me // 4
    after, before = me + 4, me - 4

    def hop(j, to, sems):
        d = j // 2
        return (
            remote(q_all.at[d], q_all.at[d], sems.at[0, j // 4], q_r.at[d], to),
            remote(kv_all.at[j], kv_all.at[j], sems.at[1, j // 4], kv_r.at[j], to),
        )

    def fw_copy(j):
        return remote(kv_all.at[j], kv_all.at[j], fw_s.at[j // 2], kv_r.at[j], partner)

    def hop_on(j, to, sems):
        for copy in hop(j, to, sems):
            copy.start()

    @pl.when(row < row_count - 1)
    def _():
        hop_on(me, after, up_s)

    @pl.when(row > 0)
    def _():
        hop_on(me, before, down_s)

    hop_on(me, across, side_s)

    def arrive(j):
        landed(q_all.at[j // 2], q_r.at[j // 2])
        landed(kv_all.at[j], kv_r.at[j])

    for k in range(1, row_count):

        @pl.when(row >= k)
        def _():
            j = me - 4 * k
            arrive(j)

            @pl.when(row < row_count - 1)
            def _():
                hop_on(j, after, up_s)

            hop_on(j, across, side_s)
            fw_copy(j).start()

        @pl.when(row + k < row_count)
        def _():
            j = me + 4 * k
            arrive(j)

            @pl.when(row > 0)
            def _():
                hop_on(j, before, down_s)

            hop_on(j, across, side_s)
            fw_copy(j).start()

    inputs[3].wait()
    for i in range(half):
        for t in range(3):
            whole = in_slot(half + i, lambda c: video_ref[t, :, c])
            whole = whole.astype(f32).reshape(n, piece, hd)
            t_send[:, t, :, i * hd : (i + 1) * hd] = whole.astype(bf16)

    lax.fori_loop(1, n, start_t, 0)
    t_recv[me] = t_send[me]
    landed(pair_video, pair_r.at[0])
    landed(pair_text, pair_r.at[1])

    def wait_q(k, c):
        j = lax.rem(across + n - 4 * k, n) // 2
        landed(q_all.at[j], q_r.at[j])
        return c

    lax.fori_loop(0, row_count, wait_q, 0)

    length = len_ref[0]
    key = lax.broadcasted_iota(jnp.int32, (1, 2 * positions + 2 * shard), 1)
    offset = key - 2 * positions
    token = jnp.where(offset < shard, me * shard + offset, partner * shard + offset - shard)
    key_ok = (offset < 0) | (token < length)
    lane = lax.broadcasted_iota(jnp.int32, (rows, 128), 1)
    stats = jnp.where(lane < 64, 0.0, 1.0).astype(f32)
    for h in range(heads):
        hs = slice(h * hd, (h + 1) * hd)
        q = q_all[:, :, hs].reshape(rows, hd)
        keys = jnp.concatenate(
            [video_ref[1, :, hs], pair_video[0, :, hs], text_ref[1, :, hs], pair_text[0, :, hs]],
            axis=0,
        )
        values = jnp.concatenate(
            [video_ref[2, :, hs], pair_video[1, :, hs], text_ref[2, :, hs], pair_text[1, :, hs]],
            axis=0,
        )
        s = jnp.where(key_ok, dot_nt(q, keys) * scale, masked_score)
        top, total, w = softmax_parts(s)
        part = dot_nn(w, values).astype(bf16).reshape(row_count, 2, shard, hd)
        for y in range(2):
            p_send[y, :, :, hs] = part[:, y]
        stats = jnp.where(lane == h, top, jnp.where(lane == h + 64, total, stats))
    stats = stats.reshape(row_count, 2, shard, 128)
    for y in range(2):
        m_send[y] = stats[:, y]

    column = lax.rem(mine, 2)
    across_copies = (
        remote(p_send.at[1 - column], p_mid, pa_s.at[0], pa_r.at[0], across),
        remote(m_send.at[1 - column], m_mid, pa_s.at[1], pa_r.at[1], across),
    )
    for copy in across_copies:
        copy.start()
    def wait_t(k, c):
        j = lax.rem(me + k, n)
        landed(t_recv.at[j], t_r.at[j])
        return c

    lax.fori_loop(1, n, wait_t, 0)
    count = n * piece
    row_at = lax.rem(lax.broadcasted_iota(jnp.int32, (count, count), 0), piece)
    col_at = lax.rem(lax.broadcasted_iota(jnp.int32, (count, count), 1), piece)
    same = row_at == col_at
    for i in range(half):
        hs = slice(i * hd, (i + 1) * hd)
        q, k_, v = (
            t_recv[:, t, :, hs].astype(f32).reshape(count, hd).astype(bf16) for t in range(3)
        )
        s = jnp.where(same, dot_nt(q, k_) * scale, masked_score)
        top, total, w = softmax_parts(s)
        o = dot_nn(w, v) / total
        o_send[:, :, hs] = o.reshape(n, piece, hd).astype(bf16)

    def o_copy(to):
        return remote(o_send.at[to], o_recv.at[me], o_s.at[to], o_r.at[me], to)

    def start_o(k, c):
        o_copy(lax.rem(me + k, n)).start()
        return c

    lax.fori_loop(1, n, start_o, 0)
    o_recv[me] = o_send[me]

    landed(p_mid, pa_r.at[0])
    landed(m_mid, pa_r.at[1])
    for z in range(row_count):
        ours, theirs = m_send[column, z], m_mid[z]
        best = jnp.maximum(ours, theirs)
        w_ours, w_theirs = jnp.exp(ours - best), jnp.exp(theirs - best)
        total = pltpu.roll(w_ours, 64, 1) * ours + pltpu.roll(w_theirs, 64, 1) * theirs
        m_out[z] = jnp.where(lax.broadcasted_iota(jnp.int32, best.shape, 1) < 64, best, total)
        for h in range(heads):
            hs = slice(h * hd, (h + 1) * hd)
            p_out[z, :, hs] = (
                w_ours[:, h : h + 1] * p_send[column, z, :, hs].astype(f32)
                + w_theirs[:, h : h + 1] * p_mid[z, :, hs].astype(f32)
            ).astype(bf16)

    def p_copy(to):
        z = to // 4
        return remote(p_out.at[z], p_recv.at[row], p_s.at[z], p_r.at[row], to)

    def m_copy(to):
        z = to // 4
        return remote(m_out.at[z], m_recv.at[row], m_s.at[z], m_r.at[row], to)

    def start_p(k, c):
        p_copy(along(k)).start()
        m_copy(along(k)).start()
        return c

    lax.fori_loop(1, row_count, start_p, 0)
    p_recv[row] = p_out[row]
    m_recv[row] = m_out[row]

    def forward(k, c):
        j = lax.rem(across + n - 4 * k, n)
        landed(kv_all.at[j], kv_r.at[j])
        fw_copy(j).start()
        return c

    lax.fori_loop(0, row_count, forward, 0)

    def wait_kv(k, c):
        j = lax.rem(partner + 2 * k, n)
        landed(kv_all.at[j], kv_r.at[j])
        return c

    lax.fori_loop(0, twins, wait_kv, 0)
    text_key = lax.broadcasted_iota(jnp.int32, (1, positions + text_total), 1) - positions
    joint_ok = text_key < length
    for i in range(half):
        q, k_, v = (in_slot(i, lambda c: video_ref[t, :, c]) for t in range(3))
        hs = slice(i * hd, (i + 1) * hd)
        keys = jnp.concatenate(
            [k_, kv_all[:, 0, :, hs].reshape(text_total, hd)], axis=0
        )
        values = jnp.concatenate(
            [v, kv_all[:, 1, :, hs].reshape(text_total, hd)], axis=0
        )
        s = jnp.where(joint_ok, dot_nt(q, keys) * scale, masked_score)
        top, total, w = softmax_parts(s)
        result[i] = (dot_nn(w, values) / total).astype(bf16)

    for h in range(heads):
        block = result[max(0, h - half)]
        for i in range(max(0, h - half) + 1, min(h, half - 1) + 1):
            block = jnp.where(places[h] == i, result[i], block)
        video_out[:, h * hd : (h + 1) * hd] = block

    def wait_p(k, c):
        j = along(k) // 4
        landed(p_recv.at[j], p_r.at[j])
        landed(m_recv.at[j], m_r.at[j])
        return c

    lax.fori_loop(1, row_count, wait_p, 0)
    tops = m_recv[...]
    sums = pltpu.roll(tops.reshape(row_count * shard, 128), 64, 1).reshape(tops.shape)
    best = tops.max(0, keepdims=True)
    weight = jnp.exp(jnp.minimum(tops - best, 0.0))
    total = (weight * sums).sum(0)
    for h in range(heads):
        hs = slice(h * hd, (h + 1) * hd)
        merged = (weight[:, :, h : h + 1] * p_recv[:, :, hs].astype(f32)).sum(0)
        text_out[:, hs] = (merged / total[:, h : h + 1]).astype(bf16)

    def wait_o(k, c):
        j = lax.rem(me + k, n)
        landed(o_recv.at[j], o_r.at[j])
        return c

    lax.fori_loop(1, n, wait_o, 0)
    for i in range(half):
        hs = slice(i * hd, (i + 1) * hd)
        result[half + i] = o_recv[:, :, hs].astype(f32).reshape(positions, hd).astype(bf16)
    for h in range(heads):
        hs = slice(h * hd, (h + 1) * hd)
        block = video_out[:, hs]
        for i in range(max(0, h - half), min(h, half - 1) + 1):
            block = jnp.where(places[h] == half + i, result[half + i], block)
        video_out[:, hs] = block

    sent(pair_video, pair_s.at[0])
    sent(pair_text, pair_s.at[1])
    sent(kv_all.at[me], fw_s.at[mine])

    for copy in across_copies:
        copy.wait_send()

    def gone(sems, j):
        sent(q_all.at[mine], sems.at[0, j])
        sent(kv_all.at[me], sems.at[1, j])

    for z in range(row_count):
        gone(side_s, z)

        @pl.when((z <= row) & (row < row_count - 1))
        def _():
            gone(up_s, z)

        @pl.when((z >= row) & (row > 0))
        def _():
            gone(down_s, z)

    def drain_row(k, c):
        j = along(k)
        sent(kv_all.at[me], fw_s.at[j // 2])
        sent(p_out.at[0], p_s.at[j // 4])
        sent(m_out.at[0], m_s.at[j // 4])
        return c

    lax.fori_loop(1, row_count, drain_row, 0)

    def drain_across(k, c):
        j = lax.rem(across + 4 * k, n)
        sent(kv_all.at[me], fw_s.at[j // 2])
        return c

    lax.fori_loop(0, row_count, drain_across, 0)

    def drain_all(k, c):
        j = lax.rem(me + k, n)
        sent(t_send.at[j], t_s.at[j])
        sent(o_send.at[j], o_s.at[j])
        return c

    lax.fori_loop(1, n, drain_all, 0)


def fused_body(n, video_qkv, text_qkv, head_kind, text_len):
    heads = head_kind.shape[0]
    _, _, positions, width = video_qkv.shape
    shard = text_qkv.shape[1]
    half, twins, piece = heads // 2, n // 2, positions // n
    hd = width // heads
    narrow = half * hd
    rows = n // 4
    vmem = pl.BlockSpec(memory_space=pltpu.VMEM)
    hbm = pl.BlockSpec(memory_space=pltpu.HBM)
    dma = pltpu.SemaphoreType.DMA
    video_out, text_out = pl.pallas_call(
        functools.partial(kernel, n, heads),
        out_shape=(
            jax.ShapeDtypeStruct((positions, width), bf16),
            jax.ShapeDtypeStruct((shard, width), bf16),
        ),
        in_specs=[hbm] * 4,
        out_specs=(vmem, vmem),
        scratch_shapes=[
            pltpu.SMEM((heads,), jnp.int32),
            pltpu.SMEM((1,), jnp.int32),
            pltpu.VMEM((3, positions, width), bf16),
            pltpu.VMEM((3, shard, width), bf16),
            pltpu.VMEM((2, positions, width), bf16),
            pltpu.VMEM((2, shard, width), bf16),
            pltpu.VMEM((twins, shard, width), bf16),
            pltpu.VMEM((n, 2, shard, narrow), bf16),
            pltpu.VMEM((n, 3, piece, narrow), bf16),
            pltpu.VMEM((n, 3, piece, narrow), bf16),
            pltpu.VMEM((n, piece, narrow), bf16),
            pltpu.VMEM((n, piece, narrow), bf16),
            pltpu.VMEM((2, rows, shard, width), bf16),
            pltpu.VMEM((rows, shard, width), bf16),
            pltpu.VMEM((rows, shard, width), bf16),
            pltpu.VMEM((rows, shard, width), bf16),
            pltpu.VMEM((2, rows, shard, 128), f32),
            pltpu.VMEM((rows, shard, 128), f32),
            pltpu.VMEM((rows, shard, 128), f32),
            pltpu.VMEM((rows, shard, 128), f32),
            pltpu.VMEM((heads, positions, hd), bf16),
            dma((4,)),
            dma((2,)),
            dma((2,)),
            dma((2, rows)),
            dma((2, rows)),
            dma((2, rows)),
            dma((twins,)),
            dma((n,)),
            dma((twins,)),
            dma((n,)),
            dma((n,)),
            dma((n,)),
            dma((n,)),
            dma((2,)),
            dma((2,)),
            dma((rows,)),
            dma((rows,)),
            dma((rows,)),
            dma((rows,)),
        ],
        compiler_params=pltpu.CompilerParams(
            collective_id=0, has_side_effects=True, vmem_limit_bytes=63 << 20
        ),
    )(head_kind, text_len, video_qkv.reshape(3, positions, width), text_qkv)
    return video_out.reshape(1, positions, width), text_out


def body(n, video_qkv, text_qkv, head_kind, text_len):
    heads = head_kind.shape[0]
    positions, width = video_qkv.shape[2:]
    shard = text_qkv.shape[1]
    whole_tiles = (
        video_qkv.shape[1] == 1
        and n % 4 == 0
        and heads % 2 == 0
        and heads <= 64
        and shard % 16 == 0
        and positions % (8 * n) == 0
        and (width // heads) % 128 == 0
    )
    if whole_tiles:
        return fused_body(n, video_qkv, text_qkv, head_kind, text_len)
    return plain_body(video_qkv, text_qkv, head_kind, text_len)


def solution(mesh):
    in_specs = (
        P(None, ("groups", "frame"), None, None),
        P(None, ("groups", "frame"), None),
        P("groups"),
        P("groups"),
    )
    out_specs = (P(("groups", "frame"), None, None), P(("groups", "frame"), None))
    return jax.shard_map(
        functools.partial(body, mesh.shape["frame"]), mesh=mesh, in_specs=in_specs, out_specs=out_specs, check_vma=False)
```

```python
import functools

import jax
import jax.numpy as jnp
from jax import lax
from jax.experimental import pallas as pl
from jax.experimental.pallas import tpu as pltpu
from jax.sharding import PartitionSpec as P

masked_score = -1e30


def plain_body(video_qkv, text_qkv, head_kind, text_len):
    head_count = head_kind.shape[0]
    head_width = video_qkv.shape[-1]
    head_dim = head_width // head_count
    positions = video_qkv.shape[2]
    shard_text = text_qkv.shape[1]
    score_scale = head_dim ** (-0.5)
    device_rank = lax.axis_index("frame")
    local_video = video_qkv.reshape(3, 1, positions, head_count, head_dim)
    gathered = lax.all_gather(text_qkv, "frame", axis=1, tiled=True)
    text_total = gathered.shape[1]
    all_text = gathered.reshape(3, text_total, head_count, head_dim)
    text_valid = jnp.arange(text_total) < text_len[0]
    spatial_heads = jnp.nonzero(head_kind == 0, size=head_count - head_count // 2)[0].astype(
        jnp.int32
    )
    temporal_heads = jnp.nonzero(head_kind == 1, size=head_count // 2)[0].astype(jnp.int32)
    own_frame = jnp.take(local_video[:, 0], spatial_heads, axis=2)
    text_spatial = jnp.take(all_text[1:], spatial_heads, axis=2)
    joint_keys = jnp.concatenate([own_frame[1], text_spatial[0]], axis=0)
    joint_values = jnp.concatenate([own_frame[2], text_spatial[1]], axis=0)
    joint_valid = jnp.concatenate([jnp.ones((positions,), bool), text_valid])
    spatial_scores = (
        jnp.einsum("phd,khd->hpk", own_frame[0], joint_keys, preferred_element_type=jnp.float32)
        * score_scale
    )
    spatial_scores = jnp.where(joint_valid, spatial_scores, masked_score)
    row_max = spatial_scores.max(-1, keepdims=True)
    spatial_exp = jnp.exp(spatial_scores - row_max)
    totals = spatial_exp.sum(-1)
    summed = jnp.einsum(
        "hpk,khd->phd",
        spatial_exp.astype(jnp.bfloat16),
        joint_values,
        preferred_element_type=jnp.float32,
    )
    spatial_result = (summed / totals.T[..., None]).astype(jnp.bfloat16)
    selected = jnp.take(local_video, temporal_heads, axis=3)
    block = lax.all_to_all(selected, "frame", split_axis=2, concat_axis=1, tiled=True)
    scores = (
        jnp.einsum("fphd,gphd->phfg", block[0], block[1], preferred_element_type=jnp.float32)
        * score_scale
    )
    block_max = scores.max(-1, keepdims=True)
    exps = jnp.exp(scores - block_max)
    block_totals = exps.sum(-1)
    block_sum = jnp.einsum(
        "phfg,gphd->fphd", exps.astype(jnp.bfloat16), block[2], preferred_element_type=jnp.float32
    )
    result = (block_sum / jnp.transpose(block_totals, (2, 0, 1))[..., None]).astype(jnp.bfloat16)
    temporal_result = lax.all_to_all(result, "frame", split_axis=0, concat_axis=1, tiled=True)[0]
    joined = jnp.concatenate([spatial_result, temporal_result], axis=1)
    order = jnp.concatenate([spatial_heads, temporal_heads])
    inverse = jnp.argsort(order)
    video_out = jnp.take(joined, inverse, axis=1).reshape(1, positions, head_width)
    text_queries = all_text[0]
    own_text = text_qkv.reshape(3, shard_text, head_count, head_dim)
    own_valid = device_rank * shard_text + jnp.arange(shard_text) < text_len[0]
    local_keys = jnp.concatenate([local_video[1, 0], own_text[1]], axis=0)
    local_values = jnp.concatenate([local_video[2, 0], own_text[2]], axis=0)
    local_valid = jnp.concatenate([jnp.ones((positions,), bool), own_valid])
    query_scores = (
        jnp.einsum("thd,khd->thk", text_queries, local_keys, preferred_element_type=jnp.float32)
        * score_scale
    )
    query_scores = jnp.where(local_valid, query_scores, masked_score)
    local_max = query_scores.max(-1)
    global_max = lax.pmax(local_max, "frame")
    query_exp = jnp.exp(query_scores - global_max[..., None])
    query_totals = query_exp.sum(-1)
    query_sums = jnp.einsum(
        "thk,khd->thd",
        query_exp.astype(jnp.bfloat16),
        local_values,
        preferred_element_type=jnp.float32,
    )
    query_totals, query_sums = (query_totals, query_sums)
    query_sums, query_totals = (
        lax.psum_scatter(query_sums, "frame", scatter_dimension=0, tiled=True),
        lax.psum_scatter(query_totals, "frame", scatter_dimension=0, tiled=True),
    )
    text_out = (
        (query_sums / query_totals[..., None]).astype(jnp.bfloat16).reshape(shard_text, head_width)
    )
    return (video_out, text_out)


f32 = jnp.float32
bf16 = jnp.bfloat16


def dot_nt(a, b):
    return lax.dot_general(a, b, (((1,), (1,)), ((), ())), preferred_element_type=f32)


def dot_nn(a, b):
    return lax.dot_general(a, b, (((1,), (0,)), ((), ())), preferred_element_type=f32)


def softmax_parts(scores):
    top = scores.max(-1, keepdims=True)
    e = jnp.exp(scores - top)
    return top, e.sum(-1, keepdims=True), e.astype(bf16)


def remote(src, dst, send_sem, recv_sem, peer):
    return pltpu.make_async_remote_copy(
        src_ref=src,
        dst_ref=dst,
        send_sem=send_sem,
        recv_sem=recv_sem,
        device_id={"frame": peer},
        device_id_type=pl.DeviceIdType.MESH,
    )


def kernel(
    n,
    heads,
    kind_hbm,
    len_hbm,
    video_hbm,
    text_hbm,
    video_out,
    text_out,
    kind_ref,
    len_ref,
    video_ref,
    text_ref,
    pair_video,
    pair_text,
    q_all,
    kv_all,
    t_send,
    t_recv,
    o_send,
    o_recv,
    p_send,
    p_mid,
    p_out,
    p_recv,
    m_send,
    m_mid,
    m_out,
    m_recv,
    result,
    in_sem,
    pair_s,
    pair_r,
    up_s,
    down_s,
    side_s,
    q_r,
    kv_r,
    fw_s,
    t_s,
    t_r,
    o_s,
    o_r,
    pa_s,
    pa_r,
    p_s,
    p_r,
    m_s,
    m_r,
):
    half = heads // 2
    twins = n // 2
    positions = video_ref.shape[1]
    hd = video_ref.shape[2] // heads
    shard = text_ref.shape[1]
    piece = positions // n
    text_total = n * shard
    rows = twins * shard
    scale = hd ** (-0.5)
    me = lax.axis_index("frame")
    parity = lax.rem(me, 2)
    across = me + 2 - 4 * lax.rem(me // 2, 2)
    row_count = n // 4
    partner = me + 1 - 2 * parity
    mine = me // 2

    barrier = pltpu.get_barrier_semaphore()

    def greet(k, c):
        pl.semaphore_signal(
            barrier,
            inc=1,
            device_id={"frame": lax.rem(me + k, n)},
            device_id_type=pl.DeviceIdType.MESH,
        )
        return c

    inputs = [
        pltpu.make_async_copy(a, b, in_sem.at[i])
        for i, (a, b) in enumerate(
            (
                (kind_hbm, kind_ref),
                (len_hbm, len_ref),
                (text_hbm, text_ref),
                (video_hbm, video_ref),
            )
        )
    ]
    for copy in inputs:
        copy.start()
    lax.fori_loop(1, n, greet, 0)
    for copy in inputs[:3]:
        copy.wait()

    spatial_seen = jnp.int32(0)
    temporal_seen = jnp.int32(0)
    places = []
    for h in range(heads):
        kind = kind_ref[h]
        place = jnp.where(kind == 0, spatial_seen, half + temporal_seen)
        places.append(place)
        spatial_seen = spatial_seen + jnp.where(kind == 0, 1, 0)
        temporal_seen = temporal_seen + jnp.where(kind == 0, 0, 1)

    def in_slot(i, load):
        first = i % half
        block = load(slice(first * hd, (first + 1) * hd))
        for h in range(first + 1, first + half + 1):
            block = jnp.where(places[h] == i, load(slice(h * hd, (h + 1) * hd)), block)
        return block

    for i in range(half):
        for t in range(2):
            kv_all[me, t, :, i * hd : (i + 1) * hd] = in_slot(i, lambda c: text_ref[t + 1, :, c])
    q_all[mine] = text_ref[0]

    pl.semaphore_wait(barrier, n - 1)

    def pair_copies():
        return (
            remote(video_hbm.at[1:3], pair_video, pair_s.at[0], pair_r.at[0], partner),
            remote(text_hbm.at[1:3], pair_text, pair_s.at[1], pair_r.at[1], partner),
            remote(kv_all.at[me], kv_all.at[me], fw_s.at[mine], kv_r.at[me], partner),
        )

    for c in pair_copies():
        c.start()

    def along(k):
        return lax.rem(me + 4 * k, n)

    def t_copy(to):
        return remote(t_send.at[to], t_recv.at[me], t_s.at[to], t_r.at[me], to)

    def landed(dst, sem):
        remote(dst, dst, sem, sem, partner).wait_recv()

    def sent(src, sem):
        remote(src, src, sem, sem, partner).wait_send()

    def start_t(k, c):
        t_copy(lax.rem(me + k, n)).start()
        return c

    row = me // 4
    after, before = me + 4, me - 4

    def hop(j, to, sems):
        d = j // 2
        return (
            remote(q_all.at[d], q_all.at[d], sems.at[0, j // 4], q_r.at[d], to),
            remote(kv_all.at[j], kv_all.at[j], sems.at[1, j // 4], kv_r.at[j], to),
        )

    def fw_copy(j):
        return remote(kv_all.at[j], kv_all.at[j], fw_s.at[j // 2], kv_r.at[j], partner)

    def hop_on(j, to, sems):
        for copy in hop(j, to, sems):
            copy.start()

    @pl.when(row < row_count - 1)
    def _():
        hop_on(me, after, up_s)

    @pl.when(row > 0)
    def _():
        hop_on(me, before, down_s)

    hop_on(me, across, side_s)

    def arrive(j):
        landed(q_all.at[j // 2], q_r.at[j // 2])
        landed(kv_all.at[j], kv_r.at[j])

    for k in range(1, row_count):

        @pl.when(row >= k)
        def _():
            j = me - 4 * k
            arrive(j)

            @pl.when(row < row_count - 1)
            def _():
                hop_on(j, after, up_s)

            hop_on(j, across, side_s)
            fw_copy(j).start()

        @pl.when(row + k < row_count)
        def _():
            j = me + 4 * k
            arrive(j)

            @pl.when(row > 0)
            def _():
                hop_on(j, before, down_s)

            hop_on(j, across, side_s)
            fw_copy(j).start()

    inputs[3].wait()
    for i in range(half):
        for t in range(3):
            whole = in_slot(half + i, lambda c: video_ref[t, :, c])
            whole = whole.astype(f32).reshape(n, piece, hd)
            t_send[:, t, :, i * hd : (i + 1) * hd] = whole.astype(bf16)

    lax.fori_loop(twins, n, start_t, 0)
    lax.fori_loop(1, twins, start_t, 0)
    t_recv[me] = t_send[me]
    landed(pair_video, pair_r.at[0])
    landed(pair_text, pair_r.at[1])

    def wait_q(k, c):
        j = lax.rem(across + n - 4 * k, n) // 2
        landed(q_all.at[j], q_r.at[j])
        return c

    lax.fori_loop(0, row_count, wait_q, 0)

    length = len_ref[0]
    key = lax.broadcasted_iota(jnp.int32, (1, 2 * positions + 2 * shard), 1)
    offset = key - 2 * positions
    token = jnp.where(offset < shard, me * shard + offset, partner * shard + offset - shard)
    key_ok = (offset < 0) | (token < length)
    lane = lax.broadcasted_iota(jnp.int32, (rows, 128), 1)
    stats = jnp.where(lane < 64, 0.0, 1.0).astype(f32)
    for h in range(heads):
        hs = slice(h * hd, (h + 1) * hd)
        q = q_all[:, :, hs].reshape(rows, hd)
        keys = jnp.concatenate(
            [video_ref[1, :, hs], pair_video[0, :, hs], text_ref[1, :, hs], pair_text[0, :, hs]],
            axis=0,
        )
        values = jnp.concatenate(
            [video_ref[2, :, hs], pair_video[1, :, hs], text_ref[2, :, hs], pair_text[1, :, hs]],
            axis=0,
        )
        s = jnp.where(key_ok, dot_nt(q, keys) * scale, masked_score)
        top, total, w = softmax_parts(s)
        part = dot_nn(w, values).astype(bf16).reshape(row_count, 2, shard, hd)
        for y in range(2):
            p_send[y, :, :, hs] = part[:, y]
        stats = jnp.where(lane == h, top, jnp.where(lane == h + 64, total, stats))
    stats = stats.reshape(row_count, 2, shard, 128)
    for y in range(2):
        m_send[y] = stats[:, y]

    column = lax.rem(mine, 2)
    across_copies = (
        remote(p_send.at[1 - column], p_mid, pa_s.at[0], pa_r.at[0], across),
        remote(m_send.at[1 - column], m_mid, pa_s.at[1], pa_r.at[1], across),
    )
    for copy in across_copies:
        copy.start()
    def wait_t(k, c):
        j = lax.rem(me + k, n)
        landed(t_recv.at[j], t_r.at[j])
        return c

    lax.fori_loop(1, n, wait_t, 0)
    count = n * piece
    row_at = lax.rem(lax.broadcasted_iota(jnp.int32, (count, count), 0), piece)
    col_at = lax.rem(lax.broadcasted_iota(jnp.int32, (count, count), 1), piece)
    same = row_at == col_at
    for i in range(half):
        hs = slice(i * hd, (i + 1) * hd)
        q, k_, v = (
            t_recv[:, t, :, hs].astype(f32).reshape(count, hd).astype(bf16) for t in range(3)
        )
        s = jnp.where(same, dot_nt(q, k_) * scale, masked_score)
        top, total, w = softmax_parts(s)
        o = dot_nn(w, v) / total
        o_send[:, :, hs] = o.reshape(n, piece, hd).astype(bf16)

    def o_copy(to):
        return remote(o_send.at[to], o_recv.at[me], o_s.at[to], o_r.at[me], to)

    def start_o(k, c):
        o_copy(lax.rem(me + k, n)).start()
        return c

    lax.fori_loop(1, n, start_o, 0)
    o_recv[me] = o_send[me]

    landed(p_mid, pa_r.at[0])
    landed(m_mid, pa_r.at[1])
    for z in range(row_count):
        ours, theirs = m_send[column, z], m_mid[z]
        best = jnp.maximum(ours, theirs)
        w_ours, w_theirs = jnp.exp(ours - best), jnp.exp(theirs - best)
        total = pltpu.roll(w_ours, 64, 1) * ours + pltpu.roll(w_theirs, 64, 1) * theirs
        m_out[z] = jnp.where(lax.broadcasted_iota(jnp.int32, best.shape, 1) < 64, best, total)
        for h in range(heads):
            hs = slice(h * hd, (h + 1) * hd)
            p_out[z, :, hs] = (
                w_ours[:, h : h + 1] * p_send[column, z, :, hs].astype(f32)
                + w_theirs[:, h : h + 1] * p_mid[z, :, hs].astype(f32)
            ).astype(bf16)

    def p_copy(to):
        z = to // 4
        return remote(p_out.at[z], p_recv.at[row], p_s.at[z], p_r.at[row], to)

    def m_copy(to):
        z = to // 4
        return remote(m_out.at[z], m_recv.at[row], m_s.at[z], m_r.at[row], to)

    def start_p(k, c):
        p_copy(along(k)).start()
        m_copy(along(k)).start()
        return c

    lax.fori_loop(1, row_count, start_p, 0)
    p_recv[row] = p_out[row]
    m_recv[row] = m_out[row]

    def forward(k, c):
        j = lax.rem(across + n - 4 * k, n)
        landed(kv_all.at[j], kv_r.at[j])
        fw_copy(j).start()
        return c

    lax.fori_loop(0, row_count, forward, 0)

    def wait_kv(k, c):
        j = lax.rem(partner + 2 * k, n)
        landed(kv_all.at[j], kv_r.at[j])
        return c

    lax.fori_loop(0, twins, wait_kv, 0)
    text_key = lax.broadcasted_iota(jnp.int32, (1, positions + text_total), 1) - positions
    joint_ok = text_key < length
    for i in range(half):
        q, k_, v = (in_slot(i, lambda c: video_ref[t, :, c]) for t in range(3))
        hs = slice(i * hd, (i + 1) * hd)
        keys = jnp.concatenate(
            [k_, kv_all[:, 0, :, hs].reshape(text_total, hd)], axis=0
        )
        values = jnp.concatenate(
            [v, kv_all[:, 1, :, hs].reshape(text_total, hd)], axis=0
        )
        s = jnp.where(joint_ok, dot_nt(q, keys) * scale, masked_score)
        top, total, w = softmax_parts(s)
        result[i] = (dot_nn(w, values) / total).astype(bf16)

    for h in range(heads):
        block = result[max(0, h - half)]
        for i in range(max(0, h - half) + 1, min(h, half - 1) + 1):
            block = jnp.where(places[h] == i, result[i], block)
        video_out[:, h * hd : (h + 1) * hd] = block

    def wait_p(k, c):
        j = along(k) // 4
        landed(p_recv.at[j], p_r.at[j])
        landed(m_recv.at[j], m_r.at[j])
        return c

    lax.fori_loop(1, row_count, wait_p, 0)
    tops = m_recv[...]
    sums = pltpu.roll(tops.reshape(row_count * shard, 128), 64, 1).reshape(tops.shape)
    best = tops.max(0, keepdims=True)
    weight = jnp.exp(jnp.minimum(tops - best, 0.0))
    total = (weight * sums).sum(0)
    for h in range(heads):
        hs = slice(h * hd, (h + 1) * hd)
        merged = (weight[:, :, h : h + 1] * p_recv[:, :, hs].astype(f32)).sum(0)
        text_out[:, hs] = (merged / total[:, h : h + 1]).astype(bf16)

    def wait_o(k, c):
        j = lax.rem(me + k, n)
        landed(o_recv.at[j], o_r.at[j])
        return c

    lax.fori_loop(1, n, wait_o, 0)
    for i in range(half):
        hs = slice(i * hd, (i + 1) * hd)
        result[half + i] = o_recv[:, :, hs].astype(f32).reshape(positions, hd).astype(bf16)
    for h in range(heads):
        hs = slice(h * hd, (h + 1) * hd)
        block = video_out[:, hs]
        for i in range(max(0, h - half), min(h, half - 1) + 1):
            block = jnp.where(places[h] == half + i, result[half + i], block)
        video_out[:, hs] = block

    sent(pair_video, pair_s.at[0])
    sent(pair_text, pair_s.at[1])
    sent(kv_all.at[me], fw_s.at[mine])

    for copy in across_copies:
        copy.wait_send()

    def gone(sems, j):
        sent(q_all.at[mine], sems.at[0, j])
        sent(kv_all.at[me], sems.at[1, j])

    for z in range(row_count):
        gone(side_s, z)

        @pl.when((z <= row) & (row < row_count - 1))
        def _():
            gone(up_s, z)

        @pl.when((z >= row) & (row > 0))
        def _():
            gone(down_s, z)

    def drain_row(k, c):
        j = along(k)
        sent(kv_all.at[me], fw_s.at[j // 2])
        sent(p_out.at[0], p_s.at[j // 4])
        sent(m_out.at[0], m_s.at[j // 4])
        return c

    lax.fori_loop(1, row_count, drain_row, 0)

    def drain_across(k, c):
        j = lax.rem(across + 4 * k, n)
        sent(kv_all.at[me], fw_s.at[j // 2])
        return c

    lax.fori_loop(0, row_count, drain_across, 0)

    def drain_all(k, c):
        j = lax.rem(me + k, n)
        sent(t_send.at[j], t_s.at[j])
        sent(o_send.at[j], o_s.at[j])
        return c

    lax.fori_loop(1, n, drain_all, 0)


def fused_body(n, video_qkv, text_qkv, head_kind, text_len):
    heads = head_kind.shape[0]
    _, _, positions, width = video_qkv.shape
    shard = text_qkv.shape[1]
    half, twins, piece = heads // 2, n // 2, positions // n
    hd = width // heads
    narrow = half * hd
    rows = n // 4
    vmem = pl.BlockSpec(memory_space=pltpu.VMEM)
    hbm = pl.BlockSpec(memory_space=pltpu.HBM)
    dma = pltpu.SemaphoreType.DMA
    video_out, text_out = pl.pallas_call(
        functools.partial(kernel, n, heads),
        out_shape=(
            jax.ShapeDtypeStruct((positions, width), bf16),
            jax.ShapeDtypeStruct((shard, width), bf16),
        ),
        in_specs=[hbm] * 4,
        out_specs=(vmem, vmem),
        scratch_shapes=[
            pltpu.SMEM((heads,), jnp.int32),
            pltpu.SMEM((1,), jnp.int32),
            pltpu.VMEM((3, positions, width), bf16),
            pltpu.VMEM((3, shard, width), bf16),
            pltpu.VMEM((2, positions, width), bf16),
            pltpu.VMEM((2, shard, width), bf16),
            pltpu.VMEM((twins, shard, width), bf16),
            pltpu.VMEM((n, 2, shard, narrow), bf16),
            pltpu.VMEM((n, 3, piece, narrow), bf16),
            pltpu.VMEM((n, 3, piece, narrow), bf16),
            pltpu.VMEM((n, piece, narrow), bf16),
            pltpu.VMEM((n, piece, narrow), bf16),
            pltpu.VMEM((2, rows, shard, width), bf16),
            pltpu.VMEM((rows, shard, width), bf16),
            pltpu.VMEM((rows, shard, width), bf16),
            pltpu.VMEM((rows, shard, width), bf16),
            pltpu.VMEM((2, rows, shard, 128), f32),
            pltpu.VMEM((rows, shard, 128), f32),
            pltpu.VMEM((rows, shard, 128), f32),
            pltpu.VMEM((rows, shard, 128), f32),
            pltpu.VMEM((heads, positions, hd), bf16),
            dma((4,)),
            dma((2,)),
            dma((2,)),
            dma((2, rows)),
            dma((2, rows)),
            dma((2, rows)),
            dma((twins,)),
            dma((n,)),
            dma((twins,)),
            dma((n,)),
            dma((n,)),
            dma((n,)),
            dma((n,)),
            dma((2,)),
            dma((2,)),
            dma((rows,)),
            dma((rows,)),
            dma((rows,)),
            dma((rows,)),
        ],
        compiler_params=pltpu.CompilerParams(
            collective_id=0, has_side_effects=True, vmem_limit_bytes=63 << 20
        ),
    )(head_kind, text_len, video_qkv.reshape(3, positions, width), text_qkv)
    return video_out.reshape(1, positions, width), text_out


def body(n, video_qkv, text_qkv, head_kind, text_len):
    heads = head_kind.shape[0]
    positions, width = video_qkv.shape[2:]
    shard = text_qkv.shape[1]
    whole_tiles = (
        video_qkv.shape[1] == 1
        and n % 4 == 0
        and heads % 2 == 0
        and heads <= 64
        and shard % 16 == 0
        and positions % (8 * n) == 0
        and (width // heads) % 128 == 0
    )
    if whole_tiles:
        return fused_body(n, video_qkv, text_qkv, head_kind, text_len)
    return plain_body(video_qkv, text_qkv, head_kind, text_len)


def solution(mesh):
    in_specs = (
        P(None, ("groups", "frame"), None, None),
        P(None, ("groups", "frame"), None),
        P("groups"),
        P("groups"),
    )
    out_specs = (P(("groups", "frame"), None, None), P(("groups", "frame"), None))
    return jax.shard_map(
        functools.partial(body, mesh.shape["frame"]), mesh=mesh, in_specs=in_specs, out_specs=out_specs, check_vma=False)
```
